256 devices in a mesh: grp: 4 (over y), tok: 64 (over z, x, core).
Axes of the slice: x: 4, y: 4, z: 8, core: 2. Of those that a mesh axis runs over, the one named last changes fastest.
Arguments:
- hidden: bfloat16 [512, 64, 1024], P('tok', 'grp'), may hold values from -6 to 6
- draft_qkv: bfloat16 [3, 512, 64, 1024], P(None, 'tok', None, 'grp'), may hold values from -4 to 4
- self_cache: bfloat16 [512, 2, 512, 1024], P('tok', None, None, 'grp'), may hold values from -4 to 4
- cross_cache: bfloat16 [512, 2, 512, 1024], P('tok', None, None, 'grp'), may hold values from -4 to 4
- parents: int32 [512, 64], P('tok'), may hold values from -1 to 62, as said below
- counts: int32 [512], P('tok'), may hold values from 32 to 64, as said below
- self_len: int32 [512], P('tok'), may hold values from 2 to 512, as said below
- enc_len: int32 [512], P('tok'), may hold values from 2 to 512, as said below
- buckets: int32 [512, 64, 64], P('tok'), may hold values from 0 to 31
- bias_table: float32 [32, 16], P(None, 'grp'), may hold values from -4 to 4
- gain_cross: float32 [1024], replicated, may hold values from 0.25 to 1.75
- gain_ffn: float32 [1024], replicated, may hold values from 0.25 to 1.75
- gain_next: float32 [1024], replicated, may hold values from 0.25 to 1.75
- w_out_self: bfloat16 [1024, 1024], P('grp', 'tok'), may hold values from -0.1875 to 0.1875
- w_query_cross: bfloat16 [1024, 1024], P('tok', 'grp'), may hold values from -1 to 1
- w_out_cross: bfloat16 [1024, 1024], P('grp', 'tok'), may hold values from -0.1875 to 0.1875
- w_gate: bfloat16 [1024, 2816], P('tok', 'grp'), may hold values from -0.1875 to 0.1875
- w_up: bfloat16 [1024, 2816], P('tok', 'grp'), may hold values from -0.1875 to 0.1875
- w_down: bfloat16 [2816, 1024], P('grp', 'tok'), may hold values from -0.109375 to 0.109375
- w_qkv: bfloat16 [1024, 3, 1024], P('tok', None, 'grp'), may hold values from -0.1875 to 0.1875
Outputs:
- out_hidden: bfloat16 [512, 64, 1024], P('tok', 'grp')
- next_qkv: bfloat16 [3, 512, 64, 1024], P(None, 'tok', None, 'grp')
The draws below stay inside these ranges and needn't reach their ends.
Inputs may be any that keep to these rules, and one draw needn't show every extreme that they name: `parents`: slot 0 of every tree has parent -1; every other slot's parent is an earlier slot. `counts`: some request fills all 64 draft slots. `self_len`: some request fills its whole cache. `enc_len`: some request has all 512 encoder positions.
All inputs are finite; a program needn't handle non-finite values.
Results may differ from the reference program's by a relative error of at most 0.025.
Values may be sent and summed in bfloat16 or wider, within the bound.
A program may use at most 64 MiB of HBM per device.

```python
import math
import jax
import jax.numpy as jnp
from jax import lax

D = 1024
H = 16
DH = 64
FF = 2816
NB = 32
DRAFT = 64
CACHE = 512
ENC = 512
REQS = 512


def draw_parents(key, part):
    raw_bits = jax.random.randint(jax.random.fold_in(key, 44), (REQS, DRAFT), 0, 1 << 20)
    slot_ids = jnp.arange(DRAFT, dtype=jnp.int32)[None, :]
    chosen = raw_bits % jnp.maximum(slot_ids, 1)
    row_ids = jnp.arange(REQS, dtype=jnp.int32)[:, None]
    chosen = jnp.where(row_ids == 0, slot_ids - 1, chosen)
    return jnp.where(slot_ids == 0, -1, chosen).astype(jnp.int32)


def draw_counts(key, part):
    drawn = jax.random.randint(jax.random.fold_in(key, 43), (REQS,), DRAFT // 2, DRAFT + 1)
    return drawn.at[0].set(DRAFT).astype(jnp.int32)


def draw_self_len(key, part):
    drawn = jax.random.randint(jax.random.fold_in(key, 41), (REQS,), 2, CACHE + 1)
    return drawn.at[0].set(CACHE).astype(jnp.int32)


def draw_enc_len(key, part):
    drawn = jax.random.randint(jax.random.fold_in(key, 42), (REQS,), 2, ENC + 1)
    return drawn.at[0].set(ENC).astype(jnp.int32)


def draw_hidden(key, part):
    own_key = jax.random.fold_in(key, 31)
    base_draw = jax.random.truncated_normal(own_key, -6.0, 6.0, (REQS, DRAFT, D), jnp.float32)
    return base_draw.astype(jnp.bfloat16)


def draw_w_query_cross(key, part):
    base_draw = jax.random.truncated_normal(jax.random.fold_in(key, 33), -4.0, 4.0, (D, D), jnp.float32) / math.sqrt(D)
    return base_draw.astype(jnp.bfloat16)


def draw_draft_qkv(key, part):
    base_draw = 0.5 * jax.random.truncated_normal(jax.random.fold_in(key, 32), -8.0, 8.0, (3, REQS, DRAFT, D), jnp.float32)
    return base_draw.astype(jnp.bfloat16)


def draw_self_cache(key, part):
    base_draw = 0.5 * jax.random.truncated_normal(jax.random.fold_in(key, 34), -8.0, 8.0, (REQS, 2, CACHE, D), jnp.float32)
    return base_draw.astype(jnp.bfloat16)


def draw_cross_cache(key, part):
    base_draw = 0.5 * jax.random.truncated_normal(jax.random.fold_in(key, 35), -8.0, 8.0, (REQS, 2, ENC, D), jnp.float32)
    return base_draw.astype(jnp.bfloat16)


def with_ends(values, key, least, largest):
    index_at = [jax.random.randint(jax.random.fold_in(key, axis), (), 0, length) for axis, length in enumerate(values.shape)]
    widest = values.shape.index(max(values.shape))
    beside = index_at[:widest] + [(index_at[widest] + 1) % values.shape[widest]] + index_at[widest + 1:]
    return values.at[tuple(index_at)].set(least).at[tuple(beside)].set(largest)


def shard_levels(stream_key, extent, pieces, low, top_value):
    level = 1.0
    for axis_at, blocks in pieces:
        draws = jax.random.uniform(jax.random.fold_in(jax.random.fold_in(stream_key, 6), axis_at), (blocks,), jnp.float32, low / len(pieces), top_value / len(pieces))
        level = level * jnp.repeat(jnp.exp(draws), extent[axis_at] // blocks).reshape((-1,) + (1,) * (len(extent) - 1 - axis_at))
    return level


def centred(key, extent, spread, limit, pieces=(), kind=jnp.bfloat16):
    values = jax.random.normal(key, extent, jnp.float32) * spread
    if len(pieces) > 0:
        values = shard_levels(key, extent, pieces, -0.22, 0.18) * values
    return jnp.clip(values, min=-limit, max=limit).astype(kind)


def setup_inputs(seed: int = 0) -> dict:
    key_of = jax.random.split(jax.random.key(seed), 21)
    hidden = draw_hidden(jax.random.fold_in(key_of[20], 71), 0)
    draft_qkv = draw_draft_qkv(jax.random.fold_in(key_of[20], 71), 0)
    self_cache = draw_self_cache(jax.random.fold_in(key_of[20], 71), 0)
    cross_cache = draw_cross_cache(jax.random.fold_in(key_of[20], 71), 0)
    parents = draw_parents(jax.random.fold_in(key_of[20], 71), 0)
    counts = draw_counts(jax.random.fold_in(key_of[20], 71), 0)
    self_len = draw_self_len(jax.random.fold_in(key_of[20], 71), 0)
    enc_len = draw_enc_len(jax.random.fold_in(key_of[20], 71), 0)
    buckets = with_ends(jax.random.randint(key_of[8], (REQS, DRAFT, DRAFT), 0, NB), jax.random.fold_in(key_of[8], 1), 0, NB - 1).astype(jnp.int32)
    bias_table = centred(key_of[9], (NB, H), 1.0, 4.0, ((1, 4),), jnp.float32)
    gain_cross = jnp.clip(1.0 + 0.15 * jax.random.normal(key_of[10], (D,), jnp.float32), 0.25, 1.75)
    gain_ffn = jnp.clip(1.0 + 0.15 * jax.random.normal(key_of[11], (D,), jnp.float32), 0.25, 1.75)
    gain_next = jnp.clip(1.0 + 0.15 * jax.random.normal(key_of[12], (D,), jnp.float32), 0.25, 1.75)
    w_out_self = centred(key_of[13], (D, D), D ** -0.5, 0.1875, ((0, 4), (1, 64)))
    w_query_cross = draw_w_query_cross(jax.random.fold_in(key_of[20], 71), 0)
    w_out_cross = centred(key_of[15], (D, D), D ** -0.5, 0.1875, ((0, 4), (1, 64)))
    w_gate = centred(key_of[16], (D, FF), D ** -0.5, 0.1875, ((0, 64), (1, 4)))
    w_up = centred(key_of[17], (D, FF), D ** -0.5, 0.1875, ((0, 64), (1, 4)))
    w_down = centred(key_of[18], (FF, D), FF ** -0.5, 0.109375, ((0, 4), (1, 64)))
    w_qkv = centred(key_of[19], (D, 3, D), D ** -0.5, 0.1875, ((0, 64), (2, 4)))
    return {"hidden": hidden, "draft_qkv": draft_qkv, "self_cache": self_cache, "cross_cache": cross_cache, "parents": parents, "counts": counts, "self_len": self_len, "enc_len": enc_len, "buckets": buckets, "bias_table": bias_table, "gain_cross": gain_cross, "gain_ffn": gain_ffn, "gain_next": gain_next, "w_out_self": w_out_self, "w_query_cross": w_query_cross, "w_out_cross": w_out_cross, "w_gate": w_gate, "w_up": w_up, "w_down": w_down, "w_qkv": w_qkv}


def ancestor_table(parent_ids):
    count_slots = parent_ids.shape[0]
    slot_ids = jnp.arange(count_slots, dtype=jnp.int32)
    ancestors = jnp.eye(count_slots, dtype=jnp.float32) + (parent_ids[:, None] == slot_ids[None, :]).astype(jnp.float32)
    for repeat in range(max(1, count_slots.bit_length())):
        ancestors = jnp.minimum(jnp.dot(ancestors, ancestors, precision=lax.Precision.HIGHEST), 1.0)
    return ancestors

def rms_scale(stream, gain_vec):
    mean_square = lax.optimization_barrier(jnp.mean(stream * stream, axis=-1, keepdims=True))
    return (stream * lax.rsqrt(mean_square + 1e-06) * gain_vec).astype(jnp.bfloat16)

def rounded_weights(values):
    return lax.optimization_barrier(values.astype(jnp.bfloat16)).astype(jnp.float32)

def draft_attention(projected, cached, parent_ids, draft_count, length, bucket_ids, bias_table):
    draft_slots = projected.shape[1]
    all_heads = bias_table.shape[1]
    head_size = projected.shape[2] // all_heads
    queries = projected[0].astype(jnp.float32).reshape(draft_slots, all_heads, head_size)
    draft_keys = projected[1].astype(jnp.float32).reshape(draft_slots, all_heads, head_size)
    draft_values = projected[2].astype(jnp.float32).reshape(draft_slots, all_heads, head_size)
    cache_keys = cached[0].astype(jnp.float32).reshape(-1, all_heads, head_size)
    cache_values = cached[1].astype(jnp.float32).reshape(-1, all_heads, head_size)
    cache_scores = jnp.einsum('ihd,phd->hip', queries, cache_keys) + bias_table[-1][:, None, None]
    cache_live = jnp.arange(cache_keys.shape[0], dtype=jnp.int32)[None, None, :] < length
    cache_scores = jnp.where(cache_live, cache_scores, -1e+30)
    draft_bias = jnp.transpose(bias_table[bucket_ids], (2, 0, 1))
    draft_scores = jnp.einsum('ihd,jhd->hij', queries, draft_keys) + draft_bias
    draft_live = (ancestor_table(parent_ids) > 0.5) & (jnp.arange(draft_slots, dtype=jnp.int32)[None, :] < draft_count)
    draft_scores = jnp.where(draft_live[None], draft_scores, -1e+30)
    highest = jnp.maximum(cache_scores.max(-1, keepdims=True), draft_scores.max(-1, keepdims=True))
    exp_cache = jnp.exp(cache_scores - highest)
    exp_draft = jnp.exp(draft_scores - highest)
    denominator = exp_cache.sum(-1, keepdims=True) + exp_draft.sum(-1, keepdims=True)
    weights_cache = rounded_weights(exp_cache / denominator)
    weights_draft = rounded_weights(exp_draft / denominator)
    attended = jnp.einsum('hip,phd->ihd', weights_cache, cache_values) + jnp.einsum('hij,jhd->ihd', weights_draft, draft_values)
    return attended.astype(jnp.bfloat16).reshape(draft_slots, -1)

def cross_attention(query_rows, cached, length):
    draft_slots = query_rows.shape[0]
    head_size = DH
    all_heads = query_rows.shape[1] // head_size
    queries = query_rows.astype(jnp.float32).reshape(draft_slots, all_heads, head_size)
    enc_keys = cached[0].astype(jnp.float32).reshape(-1, all_heads, head_size)
    enc_values = cached[1].astype(jnp.float32).reshape(-1, all_heads, head_size)
    scores = jnp.einsum('ihd,phd->hip', queries, enc_keys)
    live = jnp.arange(enc_keys.shape[0], dtype=jnp.int32)[None, None, :] < length
    scores = jnp.where(live, scores, -1e+30)
    highest = scores.max(-1, keepdims=True)
    exp_scores = jnp.exp(scores - highest)
    weights = rounded_weights(exp_scores / exp_scores.sum(-1, keepdims=True))
    attended = jnp.einsum('hip,phd->ihd', weights, enc_values)
    return attended.astype(jnp.bfloat16).reshape(draft_slots, -1)

def reference(hidden, draft_qkv, self_cache, cross_cache, parents, counts, self_len, enc_len, buckets, bias_table, gain_cross, gain_ffn, gain_next, w_out_self, w_query_cross, w_out_cross, w_gate, w_up, w_down, w_qkv):
    all_rows = REQS * DRAFT
    per_request = jnp.moveaxis(draft_qkv, 1, 0)
    self_context = lax.map(lambda request: draft_attention(request[0], request[1], request[2], request[3], request[4], request[5], bias_table), (per_request, self_cache, parents, counts, self_len, buckets))
    self_context = self_context.reshape(all_rows, D)
    stream_one = hidden.reshape(all_rows, D).astype(jnp.float32) + jnp.dot(self_context, w_out_self, preferred_element_type=jnp.float32)
    normed_one = rms_scale(stream_one, gain_cross)
    cross_query = jnp.dot(normed_one, w_query_cross, preferred_element_type=jnp.float32).astype(jnp.bfloat16)
    cross_query = cross_query.reshape(REQS, DRAFT, D)
    cross_context = lax.map(lambda request: cross_attention(request[0], request[1], request[2]), (cross_query, cross_cache, enc_len))
    cross_context = cross_context.reshape(all_rows, D)
    stream_two = stream_one + jnp.dot(cross_context, w_out_cross, preferred_element_type=jnp.float32)
    normed_two = rms_scale(stream_two, gain_ffn)
    gate_part = jnp.dot(normed_two, w_gate, preferred_element_type=jnp.float32)
    up_part = jnp.dot(normed_two, w_up, preferred_element_type=jnp.float32)
    gated = (jax.nn.gelu(gate_part, approximate=True) * up_part).astype(jnp.bfloat16)
    stream_three = stream_two + jnp.dot(gated, w_down, preferred_element_type=jnp.float32)
    out_hidden = stream_three.astype(jnp.bfloat16).reshape(REQS, DRAFT, D)
    normed_three = rms_scale(stream_three, gain_next)
    projected = jnp.dot(normed_three, w_qkv.reshape(D, 3 * D), preferred_element_type=jnp.float32).astype(jnp.bfloat16)
    next_qkv = jnp.transpose(projected.reshape(REQS, DRAFT, 3, D), (2, 0, 1, 3))
    return (out_hidden, next_qkv)
```

```python
import functools

import jax
import jax.numpy as jnp
from jax import lax
from jax.experimental import pallas as pl
from jax.experimental.pallas import tpu as pltpu
from jax.sharding import PartitionSpec as P

DH = 64


def ancestor_table(parent_ids):
    count_slots = parent_ids.shape[0]
    slot_ids = jnp.arange(count_slots, dtype=jnp.int32)
    ancestors = jnp.eye(count_slots, dtype=jnp.float32) + (
        parent_ids[:, None] == slot_ids[None, :]
    ).astype(jnp.float32)
    for repeat in range(max(1, count_slots.bit_length())):
        ancestors = jnp.minimum(jnp.dot(ancestors, ancestors, precision=lax.Precision.HIGHEST), 1.0)
    return ancestors


def rms_scale(stream, gain_vec):
    mean_square = jnp.mean(stream * stream, axis=-1, keepdims=True)
    return (stream * lax.rsqrt(mean_square + 1e-06) * gain_vec).astype(jnp.bfloat16)


def draft_attention(projected, cached, parent_ids, draft_count, length, bucket_ids, bias_table):
    requests, draft_slots, head_width = (projected.shape[1], projected.shape[2], projected.shape[3])
    local_heads = bias_table.shape[1]
    head_size = head_width // local_heads
    queries = projected[0].reshape(requests, draft_slots, local_heads, head_size)
    draft_keys = projected[1].reshape(requests, draft_slots, local_heads, head_size)
    draft_values = projected[2].reshape(requests, draft_slots, local_heads, head_size)
    cache_keys = cached[:, 0].reshape(requests, -1, local_heads, head_size)
    cache_values = cached[:, 1].reshape(requests, -1, local_heads, head_size)
    cache_scores = jnp.einsum(
        "rihd,rphd->rhip", queries, cache_keys, preferred_element_type=jnp.float32
    )
    cache_scores = cache_scores + bias_table[-1][None, :, None, None]
    cache_live = jnp.arange(cache_keys.shape[1], dtype=jnp.int32)[None, :] < length[:, None]
    cache_scores = jnp.where(cache_live[:, None, None, :], cache_scores, -1e30)
    onehot = (bucket_ids[..., None] == jnp.arange(bias_table.shape[0], dtype=jnp.int32)).astype(
        jnp.float32
    )
    draft_bias = jnp.einsum("rijb,bh->rhij", onehot, bias_table, precision=lax.Precision.HIGHEST)
    draft_scores = (
        jnp.einsum("rihd,rjhd->rhij", queries, draft_keys, preferred_element_type=jnp.float32)
        + draft_bias
    )
    ancestors = jax.vmap(ancestor_table)(parent_ids)
    draft_live = (ancestors > 0.5) & (
        jnp.arange(draft_slots, dtype=jnp.int32)[None, None, :] < draft_count[:, None, None]
    )
    draft_scores = jnp.where(draft_live[:, None], draft_scores, -1e30)
    highest = jnp.maximum(cache_scores.max(-1, keepdims=True), draft_scores.max(-1, keepdims=True))
    exp_cache = jnp.exp(cache_scores - highest)
    exp_draft = jnp.exp(draft_scores - highest)
    denominator = exp_cache.sum(-1, keepdims=True) + exp_draft.sum(-1, keepdims=True)
    weights_cache = (exp_cache / denominator).astype(jnp.bfloat16)
    weights_draft = (exp_draft / denominator).astype(jnp.bfloat16)
    attended = jnp.einsum(
        "rhip,rphd->rihd", weights_cache, cache_values, preferred_element_type=jnp.float32
    )
    attended = attended + jnp.einsum(
        "rhij,rjhd->rihd", weights_draft, draft_values, preferred_element_type=jnp.float32
    )
    return attended.astype(jnp.bfloat16).reshape(requests * draft_slots, head_width)


def cross_attention(query_rows, cached, length):
    requests, draft_slots, head_width = query_rows.shape
    local_heads = head_width // DH
    queries = query_rows.reshape(requests, draft_slots, local_heads, DH)
    enc_keys = cached[:, 0].reshape(requests, -1, local_heads, DH)
    enc_values = cached[:, 1].reshape(requests, -1, local_heads, DH)
    scores = jnp.einsum("rihd,rphd->rhip", queries, enc_keys, preferred_element_type=jnp.float32)
    live = jnp.arange(enc_keys.shape[1], dtype=jnp.int32)[None, :] < length[:, None]
    scores = jnp.where(live[:, None, None, :], scores, -1e30)
    highest = scores.max(-1, keepdims=True)
    exp_scores = jnp.exp(scores - highest)
    weights = (exp_scores / exp_scores.sum(-1, keepdims=True)).astype(jnp.bfloat16)
    attended = jnp.einsum(
        "rhip,rphd->rihd", weights, enc_values, preferred_element_type=jnp.float32
    )
    return attended.astype(jnp.bfloat16).reshape(requests * draft_slots, head_width)


def gather_kernel(n_chips, src_ref, out_ref, send_sem, recv_sem, local_sem, fwd_sem, fwd_recv_sem):
    grp = lax.axis_index("grp")
    me = lax.axis_index("tok")
    chip = me // 2
    core = me % 2
    sibling = chip * 2 + (1 - core)
    mesh_id = pl.DeviceIdType.MESH

    def peer(k):
        return lax.rem(chip + k, n_chips) * 2 + core

    barrier = pltpu.get_barrier_semaphore()
    for k in range(1, n_chips):
        pl.semaphore_signal(barrier, inc=1, device_id=(grp, peer(k)), device_id_type=mesh_id)
    pl.semaphore_signal(barrier, inc=1, device_id=(grp, sibling), device_id_type=mesh_id)
    pl.semaphore_wait(barrier, n_chips)

    local = pltpu.make_async_copy(src_ref, out_ref.at[core, chip], local_sem)
    local.start()
    for k in range(1, n_chips):
        pltpu.make_async_remote_copy(
            src_ref=src_ref,
            dst_ref=out_ref.at[core, chip],
            send_sem=send_sem,
            recv_sem=recv_sem,
            device_id=(grp, peer(k)),
            device_id_type=mesh_id,
        ).start()
    others = out_ref.at[core, pl.ds(0, n_chips - 1)]
    pltpu.make_async_copy(others, others, recv_sem).wait()
    pltpu.make_async_copy(others, others, send_sem).wait()
    local.wait()

    forward = pltpu.make_async_remote_copy(
        src_ref=out_ref.at[core],
        dst_ref=out_ref.at[core],
        send_sem=fwd_sem,
        recv_sem=fwd_recv_sem,
        device_id=(grp, sibling),
        device_id_type=mesh_id,
    )
    forward.start()
    forward.wait()


def gather_weights(block, n_tok):
    n_chips = n_tok // 2
    rows, width = block.shape
    gathered = pl.pallas_call(
        functools.partial(gather_kernel, n_chips),
        out_shape=jax.ShapeDtypeStruct((2, n_chips, rows, width), block.dtype),
        in_specs=[pl.BlockSpec(memory_space=pl.ANY)],
        out_specs=pl.BlockSpec(memory_space=pl.ANY),
        scratch_shapes=[pltpu.SemaphoreType.DMA(())] * 5,
        compiler_params=pltpu.CompilerParams(collective_id=0, has_side_effects=True),
    )(block)
    return jnp.swapaxes(gathered, 0, 1).reshape(n_tok, rows * width)


def fetch_all(n_tok, w_out_self, w_query_cross, w_out_cross, w_gate, w_up, w_down, w_qkv):
    parts = (w_out_self, w_query_cross, w_out_cross, w_gate, w_up, w_down, w_qkv)
    flat = jnp.concatenate([p.reshape(-1) for p in parts])
    width = 1024
    total = flat.shape[0]
    padded = -(-total // width) * width
    flat = jnp.pad(flat, (0, padded - total))
    gathered = gather_weights(flat.reshape(padded // width, width), n_tok)
    fetched = []
    offset = 0
    for p, column_split in zip(parts, (True, False, True, False, False, True, False)):
        size = p.size
        piece = gathered[:, offset:offset + size]
        offset += size
        if column_split:
            piece = piece.reshape((n_tok,) + p.shape)
            piece = jnp.swapaxes(piece, 0, 1).reshape(p.shape[0], n_tok * p.shape[1])
        else:
            piece = piece.reshape((n_tok * p.shape[0],) + p.shape[1:])
        fetched.append(piece)
    return tuple(fetched)


def layer_sum(summand, base_full):
    return lax.psum(summand.astype(jnp.bfloat16), "grp").astype(jnp.float32) + base_full


def normed_rows(stream, gain_vec):
    scaled = rms_scale(stream, gain_vec)
    return scaled.reshape(-1, scaled.shape[-1])


def shards(
    hidden,
    draft_qkv,
    self_cache,
    cross_cache,
    parents,
    counts,
    self_len,
    enc_len,
    buckets,
    bias_table,
    gain_cross,
    gain_ffn,
    gain_next,
    w_out_self,
    w_query_cross,
    w_out_cross,
    w_gate,
    w_up,
    w_down,
    w_qkv,
):
    requests, share_rows, model_width = hidden.shape
    draft_slots = draft_qkv.shape[2]
    head_width = draft_qkv.shape[3]
    fetched = fetch_all(
        lax.axis_size("tok"), w_out_self, w_query_cross, w_out_cross, w_gate, w_up, w_down, w_qkv
    )
    self_context = draft_attention(
        draft_qkv, self_cache, parents, counts, self_len, buckets, bias_table
    )
    partial_value = jnp.dot(self_context, fetched[0], preferred_element_type=jnp.float32)
    partial_value = partial_value.reshape(requests, draft_slots, model_width)
    own_rows = hidden.astype(jnp.float32)
    offset = lax.axis_index("grp") * share_rows
    placed = lax.dynamic_update_slice(
        jnp.zeros((requests, draft_slots, model_width), jnp.float32), own_rows, (0, offset, 0)
    )
    stream_one = layer_sum(partial_value + placed, 0.0)
    normed_one = normed_rows(stream_one, gain_cross)
    cross_query = jnp.dot(normed_one, fetched[1], preferred_element_type=jnp.float32)
    cross_query = cross_query.astype(jnp.bfloat16).reshape(requests, draft_slots, head_width)
    cross_context = cross_attention(cross_query, cross_cache, enc_len)
    partial_value = jnp.dot(cross_context, fetched[2], preferred_element_type=jnp.float32)
    stream_two = layer_sum(partial_value.reshape(requests, draft_slots, model_width), stream_one)
    normed_two = normed_rows(stream_two, gain_ffn)
    gate_part = jnp.dot(normed_two, fetched[3], preferred_element_type=jnp.float32)
    up_part = jnp.dot(normed_two, fetched[4], preferred_element_type=jnp.float32)
    gated = (jax.nn.gelu(gate_part, approximate=True) * up_part).astype(jnp.bfloat16)
    partial_value = jnp.dot(gated, fetched[5], preferred_element_type=jnp.float32)
    stream_three = layer_sum(partial_value.reshape(requests, draft_slots, model_width), stream_two)
    normed_three = normed_rows(stream_three, gain_next)
    projected = jnp.dot(
        normed_three,
        fetched[6].reshape(fetched[6].shape[0], -1),
        preferred_element_type=jnp.float32,
    )
    projected = projected.astype(jnp.bfloat16).reshape(requests, draft_slots, 3, head_width)
    next_qkv = jnp.transpose(projected, (2, 0, 1, 3))
    out_hidden = lax.dynamic_slice_in_dim(stream_three, offset, share_rows, 1).astype(jnp.bfloat16)
    return (out_hidden, next_qkv)


def solution(mesh):
    in_specs = (
        P("tok", "grp", None),
        P(None, "tok", None, "grp"),
        P("tok", None, None, "grp"),
        P("tok", None, None, "grp"),
        P("tok", None),
        P("tok"),
        P("tok"),
        P("tok"),
        P("tok", None, None),
        P(None, "grp"),
        P(),
        P(),
        P(),
        P("grp", "tok"),
        P("tok", "grp"),
        P("grp", "tok"),
        P("tok", "grp"),
        P("tok", "grp"),
        P("grp", "tok"),
        P("tok", None, "grp"),
    )
    out_specs = (P("tok", "grp", None), P(None, "tok", None, "grp"))
    return jax.shard_map(shards, mesh=mesh, in_specs=in_specs, out_specs=out_specs, check_vma=False)
```

```python
import functools

import jax
import jax.numpy as jnp
from jax import lax
from jax.experimental import pallas as pl
from jax.experimental.pallas import tpu as pltpu
from jax.sharding import PartitionSpec as P

DH = 64


def ancestor_table(parent_ids):
    count_slots = parent_ids.shape[0]
    slot_ids = jnp.arange(count_slots, dtype=jnp.int32)
    ancestors = jnp.eye(count_slots, dtype=jnp.float32) + (
        parent_ids[:, None] == slot_ids[None, :]
    ).astype(jnp.float32)
    for repeat in range(max(1, count_slots.bit_length())):
        ancestors = jnp.minimum(jnp.dot(ancestors, ancestors, precision=lax.Precision.HIGHEST), 1.0)
    return ancestors


def rms_scale(stream, gain_vec):
    mean_square = jnp.mean(stream * stream, axis=-1, keepdims=True)
    return (stream * lax.rsqrt(mean_square + 1e-06) * gain_vec).astype(jnp.bfloat16)


def draft_attention(projected, cached, parent_ids, draft_count, length, bucket_ids, bias_table):
    requests, draft_slots, head_width = (projected.shape[1], projected.shape[2], projected.shape[3])
    local_heads = bias_table.shape[1]
    head_size = head_width // local_heads
    queries = projected[0].reshape(requests, draft_slots, local_heads, head_size)
    draft_keys = projected[1].reshape(requests, draft_slots, local_heads, head_size)
    draft_values = projected[2].reshape(requests, draft_slots, local_heads, head_size)
    cache_keys = cached[:, 0].reshape(requests, -1, local_heads, head_size)
    cache_values = cached[:, 1].reshape(requests, -1, local_heads, head_size)
    cache_scores = jnp.einsum(
        "rihd,rphd->rhip", queries, cache_keys, preferred_element_type=jnp.float32
    )
    cache_scores = cache_scores + bias_table[-1][None, :, None, None]
    cache_live = jnp.arange(cache_keys.shape[1], dtype=jnp.int32)[None, :] < length[:, None]
    cache_scores = jnp.where(cache_live[:, None, None, :], cache_scores, -1e30)
    onehot = (bucket_ids[..., None] == jnp.arange(bias_table.shape[0], dtype=jnp.int32)).astype(
        jnp.float32
    )
    draft_bias = jnp.einsum("rijb,bh->rhij", onehot, bias_table, precision=lax.Precision.HIGHEST)
    draft_scores = (
        jnp.einsum("rihd,rjhd->rhij", queries, draft_keys, preferred_element_type=jnp.float32)
        + draft_bias
    )
    ancestors = jax.vmap(ancestor_table)(parent_ids)
    draft_live = (ancestors > 0.5) & (
        jnp.arange(draft_slots, dtype=jnp.int32)[None, None, :] < draft_count[:, None, None]
    )
    draft_scores = jnp.where(draft_live[:, None], draft_scores, -1e30)
    highest = jnp.maximum(cache_scores.max(-1, keepdims=True), draft_scores.max(-1, keepdims=True))
    exp_cache = jnp.exp(cache_scores - highest)
    exp_draft = jnp.exp(draft_scores - highest)
    denominator = exp_cache.sum(-1, keepdims=True) + exp_draft.sum(-1, keepdims=True)
    weights_cache = (exp_cache / denominator).astype(jnp.bfloat16)
    weights_draft = (exp_draft / denominator).astype(jnp.bfloat16)
    attended = jnp.einsum(
        "rhip,rphd->rihd", weights_cache, cache_values, preferred_element_type=jnp.float32
    )
    attended = attended + jnp.einsum(
        "rhij,rjhd->rihd", weights_draft, draft_values, preferred_element_type=jnp.float32
    )
    return attended.astype(jnp.bfloat16).reshape(requests * draft_slots, head_width)


def cross_attention(query_rows, cached, length):
    requests, draft_slots, head_width = query_rows.shape
    local_heads = head_width // DH
    queries = query_rows.reshape(requests, draft_slots, local_heads, DH)
    enc_keys = cached[:, 0].reshape(requests, -1, local_heads, DH)
    enc_values = cached[:, 1].reshape(requests, -1, local_heads, DH)
    scores = jnp.einsum("rihd,rphd->rhip", queries, enc_keys, preferred_element_type=jnp.float32)
    live = jnp.arange(enc_keys.shape[1], dtype=jnp.int32)[None, :] < length[:, None]
    scores = jnp.where(live[:, None, None, :], scores, -1e30)
    highest = scores.max(-1, keepdims=True)
    exp_scores = jnp.exp(scores - highest)
    weights = (exp_scores / exp_scores.sum(-1, keepdims=True)).astype(jnp.bfloat16)
    attended = jnp.einsum(
        "rhip,rphd->rihd", weights, enc_values, preferred_element_type=jnp.float32
    )
    return attended.astype(jnp.bfloat16).reshape(requests * draft_slots, head_width)


def gather_kernel(n_chips, src_ref, out_ref, send_sem, recv_sem, local_sem, fwd_sem, fwd_recv_sem):
    grp = lax.axis_index("grp")
    me = lax.axis_index("tok")
    chip = me // 2
    core = me % 2
    sibling = chip * 2 + (1 - core)
    mesh_id = pl.DeviceIdType.MESH

    def peer(k):
        return lax.rem(chip + k, n_chips) * 2 + core

    barrier = pltpu.get_barrier_semaphore()
    for k in range(1, n_chips):
        pl.semaphore_signal(barrier, inc=1, device_id=(grp, peer(k)), device_id_type=mesh_id)
    pl.semaphore_signal(barrier, inc=1, device_id=(grp, sibling), device_id_type=mesh_id)
    pl.semaphore_wait(barrier, n_chips)

    local = pltpu.make_async_copy(src_ref, out_ref.at[core, chip], local_sem)
    local.start()
    for k in range(1, n_chips):
        pltpu.make_async_remote_copy(
            src_ref=src_ref,
            dst_ref=out_ref.at[core, chip],
            send_sem=send_sem,
            recv_sem=recv_sem,
            device_id=(grp, peer(k)),
            device_id_type=mesh_id,
        ).start()
    others = out_ref.at[core, pl.ds(0, n_chips - 1)]
    pltpu.make_async_copy(others, others, recv_sem).wait()
    pltpu.make_async_copy(others, others, send_sem).wait()
    local.wait()

    forward = pltpu.make_async_remote_copy(
        src_ref=out_ref.at[core],
        dst_ref=out_ref.at[core],
        send_sem=fwd_sem,
        recv_sem=fwd_recv_sem,
        device_id=(grp, sibling),
        device_id_type=mesh_id,
    )
    forward.start()
    forward.wait()


def gather_weights(block, n_tok, collective_id):
    n_chips = n_tok // 2
    rows, width = block.shape
    moved = 2 * n_tok * rows * width * block.dtype.itemsize
    gathered = pl.pallas_call(
        functools.partial(gather_kernel, n_chips),
        out_shape=jax.ShapeDtypeStruct((2, n_chips, rows, width), block.dtype),
        in_specs=[pl.BlockSpec(memory_space=pl.ANY)],
        out_specs=pl.BlockSpec(memory_space=pl.ANY),
        scratch_shapes=[pltpu.SemaphoreType.DMA(())] * 5,
        compiler_params=pltpu.CompilerParams(collective_id=collective_id, has_side_effects=True),
        cost_estimate=pl.CostEstimate(flops=0, transcendentals=0, bytes_accessed=moved),
    )(block)
    return jnp.swapaxes(gathered, 0, 1).reshape(n_tok, rows * width)


def fetch_group(n_tok, collective_id, parts, column_split, after):
    flat = jnp.concatenate([p.reshape(-1) for p in parts])
    flat, _ = lax.optimization_barrier((flat, after))
    width = 1024
    total = flat.shape[0]
    padded = -(-total // width) * width
    flat = jnp.pad(flat, (0, padded - total))
    gathered = gather_weights(flat.reshape(padded // width, width), n_tok, collective_id)
    fetched = []
    offset = 0
    for p, split in zip(parts, column_split):
        size = p.size
        piece = gathered[:, offset:offset + size]
        offset += size
        if split:
            piece = piece.reshape((n_tok,) + p.shape)
            piece = jnp.swapaxes(piece, 0, 1).reshape(p.shape[0], n_tok * p.shape[1])
        else:
            piece = piece.reshape((n_tok * p.shape[0],) + p.shape[1:])
        fetched.append(piece)
    return fetched

def layer_sum(summand, base_full):
    return lax.psum(summand.astype(jnp.bfloat16), "grp").astype(jnp.float32) + base_full


def normed_rows(stream, gain_vec):
    scaled = rms_scale(stream, gain_vec)
    return scaled.reshape(-1, scaled.shape[-1])


def shards(
    hidden,
    draft_qkv,
    self_cache,
    cross_cache,
    parents,
    counts,
    self_len,
    enc_len,
    buckets,
    bias_table,
    gain_cross,
    gain_ffn,
    gain_next,
    w_out_self,
    w_query_cross,
    w_out_cross,
    w_gate,
    w_up,
    w_down,
    w_qkv,
):
    requests, share_rows, model_width = hidden.shape
    draft_slots = draft_qkv.shape[2]
    head_width = draft_qkv.shape[3]
    self_context = draft_attention(
        draft_qkv, self_cache, parents, counts, self_len, buckets, bias_table
    )
    (w_out_self_full,) = fetch_group(lax.axis_size("tok"), 3, (w_out_self,), (True,), self_context)
    partial_value = jnp.dot(self_context, w_out_self_full, preferred_element_type=jnp.float32)
    partial_value = partial_value.reshape(requests, draft_slots, model_width)
    own_rows = hidden.astype(jnp.float32)
    offset = lax.axis_index("grp") * share_rows
    placed = lax.dynamic_update_slice(
        jnp.zeros((requests, draft_slots, model_width), jnp.float32), own_rows, (0, offset, 0)
    )
    summand = partial_value + placed
    n_tok = lax.axis_size("tok")
    w_query_full, w_out_cross_full, w_gate_full = fetch_group(
        n_tok, 0, (w_query_cross, w_out_cross, w_gate), (False, True, False), summand
    )
    stream_one = layer_sum(summand, 0.0)
    normed_one = normed_rows(stream_one, gain_cross)
    cross_query = jnp.dot(normed_one, w_query_full, preferred_element_type=jnp.float32)
    cross_query = cross_query.astype(jnp.bfloat16).reshape(requests, draft_slots, head_width)
    cross_context = cross_attention(cross_query, cross_cache, enc_len)
    partial_value = jnp.dot(cross_context, w_out_cross_full, preferred_element_type=jnp.float32)
    w_up_full, w_down_full = fetch_group(n_tok, 1, (w_up, w_down), (False, True), partial_value)
    stream_two = layer_sum(partial_value.reshape(requests, draft_slots, model_width), stream_one)
    normed_two = normed_rows(stream_two, gain_ffn)
    gate_part = jnp.dot(normed_two, w_gate_full, preferred_element_type=jnp.float32)
    up_part = jnp.dot(normed_two, w_up_full, preferred_element_type=jnp.float32)
    gated = (jax.nn.gelu(gate_part, approximate=True) * up_part).astype(jnp.bfloat16)
    partial_value = jnp.dot(gated, w_down_full, preferred_element_type=jnp.float32)
    (w_qkv_full,) = fetch_group(n_tok, 2, (w_qkv,), (False,), partial_value)
    stream_three = layer_sum(partial_value.reshape(requests, draft_slots, model_width), stream_two)
    normed_three = normed_rows(stream_three, gain_next)
    projected = jnp.dot(
        normed_three,
        w_qkv_full.reshape(w_qkv_full.shape[0], -1),
        preferred_element_type=jnp.float32,
    )
    projected = projected.astype(jnp.bfloat16).reshape(requests, draft_slots, 3, head_width)
    next_qkv = jnp.transpose(projected, (2, 0, 1, 3))
    out_hidden = lax.dynamic_slice_in_dim(stream_three, offset, share_rows, 1).astype(jnp.bfloat16)
    return (out_hidden, next_qkv)


def solution(mesh):
    in_specs = (
        P("tok", "grp", None),
        P(None, "tok", None, "grp"),
        P("tok", None, None, "grp"),
        P("tok", None, None, "grp"),
        P("tok", None),
        P("tok"),
        P("tok"),
        P("tok"),
        P("tok", None, None),
        P(None, "grp"),
        P(),
        P(),
        P(),
        P("grp", "tok"),
        P("tok", "grp"),
        P("grp", "tok"),
        P("tok", "grp"),
        P("tok", "grp"),
        P("grp", "tok"),
        P("tok", None, "grp"),
    )
    out_specs = (P("tok", "grp", None), P(None, "tok", None, "grp"))
    return jax.shard_map(shards, mesh=mesh, in_specs=in_specs, out_specs=out_specs, check_vma=False)
```

```python
import functools

import jax
import jax.numpy as jnp
from jax import lax
from jax.experimental import pallas as pl
from jax.experimental.pallas import tpu as pltpu
from jax.sharding import PartitionSpec as P

DH = 64


def ancestor_table(parent_ids):
    count_slots = parent_ids.shape[0]
    slot_ids = jnp.arange(count_slots, dtype=jnp.int32)
    ancestors = jnp.eye(count_slots, dtype=jnp.float32) + (
        parent_ids[:, None] == slot_ids[None, :]
    ).astype(jnp.float32)
    for repeat in range(max(1, count_slots.bit_length())):
        ancestors = jnp.minimum(jnp.dot(ancestors, ancestors, precision=lax.Precision.HIGHEST), 1.0)
    return ancestors


def rms_scale(stream, gain_vec):
    mean_square = jnp.mean(stream * stream, axis=-1, keepdims=True)
    return (stream * lax.rsqrt(mean_square + 1e-06) * gain_vec).astype(jnp.bfloat16)


def draft_attention(projected, cached, parent_ids, draft_count, length, bucket_ids, bias_table):
    requests, draft_slots, head_width = (projected.shape[1], projected.shape[2], projected.shape[3])
    local_heads = bias_table.shape[1]
    head_size = head_width // local_heads
    queries = projected[0].reshape(requests, draft_slots, local_heads, head_size)
    draft_keys = projected[1].reshape(requests, draft_slots, local_heads, head_size)
    draft_values = projected[2].reshape(requests, draft_slots, local_heads, head_size)
    cache_keys = cached[:, 0].reshape(requests, -1, local_heads, head_size)
    cache_values = cached[:, 1].reshape(requests, -1, local_heads, head_size)
    cache_scores = jnp.einsum(
        "rihd,rphd->rhip", queries, cache_keys, preferred_element_type=jnp.float32
    )
    cache_scores = cache_scores + bias_table[-1][None, :, None, None]
    cache_live = jnp.arange(cache_keys.shape[1], dtype=jnp.int32)[None, :] < length[:, None]
    cache_scores = jnp.where(cache_live[:, None, None, :], cache_scores, -1e30)
    onehot = (bucket_ids[..., None] == jnp.arange(bias_table.shape[0], dtype=jnp.int32)).astype(
        jnp.float32
    )
    draft_bias = jnp.einsum("rijb,bh->rhij", onehot, bias_table, precision=lax.Precision.HIGHEST)
    draft_scores = (
        jnp.einsum("rihd,rjhd->rhij", queries, draft_keys, preferred_element_type=jnp.float32)
        + draft_bias
    )
    ancestors = jax.vmap(ancestor_table)(parent_ids)
    draft_live = (ancestors > 0.5) & (
        jnp.arange(draft_slots, dtype=jnp.int32)[None, None, :] < draft_count[:, None, None]
    )
    draft_scores = jnp.where(draft_live[:, None], draft_scores, -1e30)
    highest = jnp.maximum(cache_scores.max(-1, keepdims=True), draft_scores.max(-1, keepdims=True))
    exp_cache = jnp.exp(cache_scores - highest)
    exp_draft = jnp.exp(draft_scores - highest)
    denominator = exp_cache.sum(-1, keepdims=True) + exp_draft.sum(-1, keepdims=True)
    weights_cache = (exp_cache / denominator).astype(jnp.bfloat16)
    weights_draft = (exp_draft / denominator).astype(jnp.bfloat16)
    attended = jnp.einsum(
        "rhip,rphd->rihd", weights_cache, cache_values, preferred_element_type=jnp.float32
    )
    attended = attended + jnp.einsum(
        "rhij,rjhd->rihd", weights_draft, draft_values, preferred_element_type=jnp.float32
    )
    return attended.astype(jnp.bfloat16).reshape(requests * draft_slots, head_width)


def cross_attention(query_rows, cached, length):
    requests, draft_slots, head_width = query_rows.shape
    local_heads = head_width // DH
    queries = query_rows.reshape(requests, draft_slots, local_heads, DH)
    enc_keys = cached[:, 0].reshape(requests, -1, local_heads, DH)
    enc_values = cached[:, 1].reshape(requests, -1, local_heads, DH)
    scores = jnp.einsum("rihd,rphd->rhip", queries, enc_keys, preferred_element_type=jnp.float32)
    live = jnp.arange(enc_keys.shape[1], dtype=jnp.int32)[None, :] < length[:, None]
    scores = jnp.where(live[:, None, None, :], scores, -1e30)
    highest = scores.max(-1, keepdims=True)
    exp_scores = jnp.exp(scores - highest)
    weights = (exp_scores / exp_scores.sum(-1, keepdims=True)).astype(jnp.bfloat16)
    attended = jnp.einsum(
        "rhip,rphd->rihd", weights, enc_values, preferred_element_type=jnp.float32
    )
    return attended.astype(jnp.bfloat16).reshape(requests * draft_slots, head_width)


def gather_kernel(n_chips, n_in, *refs):
    srcs = refs[:n_in]
    outs = refs[n_in:2 * n_in]
    send_sems, recv_sems, local_sems, fwd_send, fwd_recv = refs[2 * n_in:]
    grp = lax.axis_index("grp")
    me = lax.axis_index("tok")
    chip = me // 2
    core = me % 2
    sibling = chip * 2 + (1 - core)
    mesh_id = pl.DeviceIdType.MESH

    barrier = pltpu.get_barrier_semaphore()
    for k in range(1, n_chips):
        peer = lax.rem(chip + k, n_chips) * 2 + core
        pl.semaphore_signal(barrier, inc=1, device_id=(grp, peer), device_id_type=mesh_id)
    pl.semaphore_signal(barrier, inc=1, device_id=(grp, sibling), device_id_type=mesh_id)
    pl.semaphore_wait(barrier, n_chips)

    locals_ = [
        pltpu.make_async_copy(srcs[i], outs[i].at[chip, core], local_sems.at[i]) for i in range(n_in)
    ]
    for copy in locals_:
        copy.start()

    def remote(i, k):
        other = lax.rem(chip + k, n_chips)
        return pltpu.make_async_remote_copy(
            src_ref=srcs[i],
            dst_ref=outs[i].at[chip, core],
            send_sem=send_sems.at[i, k],
            recv_sem=recv_sems.at[i, chip],
            device_id=(grp, other * 2 + core),
            device_id_type=mesh_id,
        )

    def send(k, carry):
        for i in range(n_in):
            remote(i, k).start()
        return carry

    lax.fori_loop(1, n_chips, send, 0)

    def arrive(k, carry):
        other = lax.rem(chip + k, n_chips)
        for i in range(n_in):
            remote(i, k).wait_send()
            pltpu.make_async_copy(
                srcs[i], outs[i].at[other, core], recv_sems.at[i, other]
            ).wait()
        return carry

    lax.fori_loop(1, n_chips, arrive, 0)
    for copy in locals_:
        copy.wait()

    def forward(i, c):
        return pltpu.make_async_remote_copy(
            src_ref=outs[i].at[c, core],
            dst_ref=outs[i].at[c, core],
            send_sem=fwd_send.at[i, c],
            recv_sem=fwd_recv.at[i, c],
            device_id=(grp, sibling),
            device_id_type=mesh_id,
        )

    def push(c, carry):
        for i in range(n_in):
            forward(i, c).start()
        return carry

    lax.fori_loop(0, n_chips, push, 0)

    def land(c, carry):
        for i in range(n_in):
            forward(i, c).wait_send()
            pltpu.make_async_copy(
                outs[i].at[c, core], outs[i].at[c, 1 - core], fwd_recv.at[i, c]
            ).wait()
        return carry

    lax.fori_loop(0, n_chips, land, 0)


def fetch_group(n_tok, collective_id, parts, after):
    parts = list(lax.optimization_barrier((tuple(parts), after))[0])
    n_chips = n_tok // 2
    n_in = len(parts)
    moved = 2 * n_tok * sum(p.size for p in parts) * parts[0].dtype.itemsize
    gathered = pl.pallas_call(
        functools.partial(gather_kernel, n_chips, n_in),
        out_shape=tuple(
            jax.ShapeDtypeStruct((n_chips, 2) + p.shape, p.dtype) for p in parts
        ),
        in_specs=[pl.BlockSpec(memory_space=pl.ANY)] * n_in,
        out_specs=tuple(pl.BlockSpec(memory_space=pl.ANY) for _ in parts),
        scratch_shapes=[
            pltpu.SemaphoreType.DMA((n_in, n_chips)),
            pltpu.SemaphoreType.DMA((n_in, n_chips)),
            pltpu.SemaphoreType.DMA((n_in,)),
            pltpu.SemaphoreType.DMA((n_in, n_chips)),
            pltpu.SemaphoreType.DMA((n_in, n_chips)),
        ],
        compiler_params=pltpu.CompilerParams(collective_id=collective_id, has_side_effects=True),
        cost_estimate=pl.CostEstimate(flops=0, transcendentals=0, bytes_accessed=moved),
    )(*parts)
    return [g.reshape((n_tok * g.shape[2],) + g.shape[3:]) for g in gathered]

def layer_sum(summand, base_full):
    return lax.psum(summand.astype(jnp.bfloat16), "grp").astype(jnp.float32) + base_full


def normed_rows(stream, gain_vec):
    scaled = rms_scale(stream, gain_vec)
    return scaled.reshape(-1, scaled.shape[-1])


def shards(
    hidden,
    draft_qkv,
    self_cache,
    cross_cache,
    parents,
    counts,
    self_len,
    enc_len,
    buckets,
    bias_table,
    gain_cross,
    gain_ffn,
    gain_next,
    w_out_self,
    w_query_cross,
    w_out_cross,
    w_gate,
    w_up,
    w_down,
    w_qkv,
):
    requests, share_rows, model_width = hidden.shape
    draft_slots = draft_qkv.shape[2]
    head_width = draft_qkv.shape[3]
    self_context = draft_attention(
        draft_qkv, self_cache, parents, counts, self_len, buckets, bias_table
    )
    (w_out_self_t,) = fetch_group(lax.axis_size("tok"), 3, (w_out_self.T,), self_context)
    partial_value = jnp.einsum(
        "rk,ok->ro", self_context, w_out_self_t, preferred_element_type=jnp.float32
    )
    partial_value = partial_value.reshape(requests, draft_slots, model_width)
    own_rows = hidden.astype(jnp.float32)
    offset = lax.axis_index("grp") * share_rows
    placed = lax.dynamic_update_slice(
        jnp.zeros((requests, draft_slots, model_width), jnp.float32), own_rows, (0, offset, 0)
    )
    summand = partial_value + placed
    n_tok = lax.axis_size("tok")
    w_query_full, w_out_cross_t, w_gate_full = fetch_group(
        n_tok, 0, (w_query_cross, w_out_cross.T, w_gate), summand
    )
    stream_one = layer_sum(summand, 0.0)
    normed_one = normed_rows(stream_one, gain_cross)
    cross_query = jnp.dot(normed_one, w_query_full, preferred_element_type=jnp.float32)
    cross_query = cross_query.astype(jnp.bfloat16).reshape(requests, draft_slots, head_width)
    cross_context = cross_attention(cross_query, cross_cache, enc_len)
    partial_value = jnp.einsum(
        "rk,ok->ro", cross_context, w_out_cross_t, preferred_element_type=jnp.float32
    )
    w_up_full, w_down_t = fetch_group(n_tok, 1, (w_up, w_down.T), partial_value)
    stream_two = layer_sum(partial_value.reshape(requests, draft_slots, model_width), stream_one)
    normed_two = normed_rows(stream_two, gain_ffn)
    gate_part = jnp.dot(normed_two, w_gate_full, preferred_element_type=jnp.float32)
    up_part = jnp.dot(normed_two, w_up_full, preferred_element_type=jnp.float32)
    gated = (jax.nn.gelu(gate_part, approximate=True) * up_part).astype(jnp.bfloat16)
    partial_value = jnp.einsum("rk,ok->ro", gated, w_down_t, preferred_element_type=jnp.float32)
    (w_qkv_full,) = fetch_group(
        n_tok, 2, (w_qkv.reshape(w_qkv.shape[0], -1),), partial_value
    )
    stream_three = layer_sum(partial_value.reshape(requests, draft_slots, model_width), stream_two)
    normed_three = normed_rows(stream_three, gain_next)
    projected = jnp.dot(
        normed_three,
        w_qkv_full.reshape(w_qkv_full.shape[0], -1),
        preferred_element_type=jnp.float32,
    )
    projected = projected.astype(jnp.bfloat16).reshape(requests, draft_slots, 3, head_width)
    next_qkv = jnp.transpose(projected, (2, 0, 1, 3))
    out_hidden = lax.dynamic_slice_in_dim(stream_three, offset, share_rows, 1).astype(jnp.bfloat16)
    return (out_hidden, next_qkv)


def solution(mesh):
    in_specs = (
        P("tok", "grp", None),
        P(None, "tok", None, "grp"),
        P("tok", None, None, "grp"),
        P("tok", None, None, "grp"),
        P("tok", None),
        P("tok"),
        P("tok"),
        P("tok"),
        P("tok", None, None),
        P(None, "grp"),
        P(),
        P(),
        P(),
        P("grp", "tok"),
        P("tok", "grp"),
        P("grp", "tok"),
        P("tok", "grp"),
        P("tok", "grp"),
        P("grp", "tok"),
        P("tok", None, "grp"),
    )
    out_specs = (P("tok", "grp", None), P(None, "tok", None, "grp"))
    return jax.shard_map(shards, mesh=mesh, in_specs=in_specs, out_specs=out_specs, check_vma=False)
```

```python
import functools

import jax
import jax.numpy as jnp
from jax import lax
from jax.experimental import pallas as pl
from jax.experimental.pallas import tpu as pltpu
from jax.sharding import PartitionSpec as P

DH = 64


def ancestor_table(parent_ids):
    count_slots = parent_ids.shape[0]
    slot_ids = jnp.arange(count_slots, dtype=jnp.int32)
    ancestors = jnp.eye(count_slots, dtype=jnp.float32) + (
        parent_ids[:, None] == slot_ids[None, :]
    ).astype(jnp.float32)
    for repeat in range(max(1, count_slots.bit_length())):
        ancestors = jnp.minimum(jnp.dot(ancestors, ancestors, precision=lax.Precision.HIGHEST), 1.0)
    return ancestors


def rms_scale(stream, gain_vec):
    mean_square = jnp.mean(stream * stream, axis=-1, keepdims=True)
    return (stream * lax.rsqrt(mean_square + 1e-06) * gain_vec).astype(jnp.bfloat16)


def draft_attention(projected, cached, parent_ids, draft_count, length, bucket_ids, bias_table):
    requests, draft_slots, head_width = (projected.shape[1], projected.shape[2], projected.shape[3])
    local_heads = bias_table.shape[1]
    head_size = head_width // local_heads
    queries = projected[0].reshape(requests, draft_slots, local_heads, head_size)
    draft_keys = projected[1].reshape(requests, draft_slots, local_heads, head_size)
    draft_values = projected[2].reshape(requests, draft_slots, local_heads, head_size)
    cache_keys = cached[:, 0].reshape(requests, -1, local_heads, head_size)
    cache_values = cached[:, 1].reshape(requests, -1, local_heads, head_size)
    cache_scores = jnp.einsum(
        "rihd,rphd->rhip", queries, cache_keys, preferred_element_type=jnp.float32
    )
    cache_scores = cache_scores + bias_table[-1][None, :, None, None]
    cache_live = jnp.arange(cache_keys.shape[1], dtype=jnp.int32)[None, :] < length[:, None]
    cache_scores = jnp.where(cache_live[:, None, None, :], cache_scores, -1e30)
    onehot = (bucket_ids[..., None] == jnp.arange(bias_table.shape[0], dtype=jnp.int32)).astype(
        jnp.float32
    )
    draft_bias = jnp.einsum("rijb,bh->rhij", onehot, bias_table, precision=lax.Precision.HIGHEST)
    draft_scores = (
        jnp.einsum("rihd,rjhd->rhij", queries, draft_keys, preferred_element_type=jnp.float32)
        + draft_bias
    )
    ancestors = jax.vmap(ancestor_table)(parent_ids)
    draft_live = (ancestors > 0.5) & (
        jnp.arange(draft_slots, dtype=jnp.int32)[None, None, :] < draft_count[:, None, None]
    )
    draft_scores = jnp.where(draft_live[:, None], draft_scores, -1e30)
    highest = jnp.maximum(cache_scores.max(-1, keepdims=True), draft_scores.max(-1, keepdims=True))
    exp_cache = jnp.exp(cache_scores - highest)
    exp_draft = jnp.exp(draft_scores - highest)
    denominator = exp_cache.sum(-1, keepdims=True) + exp_draft.sum(-1, keepdims=True)
    weights_cache = (exp_cache / denominator).astype(jnp.bfloat16)
    weights_draft = (exp_draft / denominator).astype(jnp.bfloat16)
    attended = jnp.einsum(
        "rhip,rphd->rihd", weights_cache, cache_values, preferred_element_type=jnp.float32
    )
    attended = attended + jnp.einsum(
        "rhij,rjhd->rihd", weights_draft, draft_values, preferred_element_type=jnp.float32
    )
    return attended.astype(jnp.bfloat16).reshape(requests * draft_slots, head_width)


def cross_attention(query_rows, cached, length):
    requests, draft_slots, head_width = query_rows.shape
    local_heads = head_width // DH
    queries = query_rows.reshape(requests, draft_slots, local_heads, DH)
    enc_keys = cached[:, 0].reshape(requests, -1, local_heads, DH)
    enc_values = cached[:, 1].reshape(requests, -1, local_heads, DH)
    scores = jnp.einsum("rihd,rphd->rhip", queries, enc_keys, preferred_element_type=jnp.float32)
    live = jnp.arange(enc_keys.shape[1], dtype=jnp.int32)[None, :] < length[:, None]
    scores = jnp.where(live[:, None, None, :], scores, -1e30)
    highest = scores.max(-1, keepdims=True)
    exp_scores = jnp.exp(scores - highest)
    weights = (exp_scores / exp_scores.sum(-1, keepdims=True)).astype(jnp.bfloat16)
    attended = jnp.einsum(
        "rhip,rphd->rihd", weights, enc_values, preferred_element_type=jnp.float32
    )
    return attended.astype(jnp.bfloat16).reshape(requests * draft_slots, head_width)


def gather_kernel(n_chips, n_in, n_grp, *refs):
    srcs = refs[:n_in]
    if n_grp:
        summand = refs[n_in]
        outs = refs[n_in + 1:2 * n_in + 1]
        summed = refs[2 * n_in + 1]
        rest = refs[2 * n_in + 2:]
        send_sems, recv_sems, local_sems, fwd_send, fwd_recv, parts_in, rs_send, rs_recv, ag_send, ag_recv = rest
    else:
        outs = refs[n_in:2 * n_in]
        send_sems, recv_sems, local_sems, fwd_send, fwd_recv = refs[2 * n_in:]
    grp = lax.axis_index("grp")
    me = lax.axis_index("tok")
    chip = me // 2
    core = me % 2
    sibling = chip * 2 + (1 - core)
    mesh_id = pl.DeviceIdType.MESH

    barrier = pltpu.get_barrier_semaphore()
    for k in range(1, n_chips):
        peer = lax.rem(chip + k, n_chips) * 2 + core
        pl.semaphore_signal(barrier, inc=1, device_id=(grp, peer), device_id_type=mesh_id)
    pl.semaphore_signal(barrier, inc=1, device_id=(grp, sibling), device_id_type=mesh_id)
    for j in range(1, max(n_grp, 1)):
        pl.semaphore_signal(
            barrier, inc=1, device_id=(lax.rem(grp + j, n_grp), me), device_id_type=mesh_id
        )
    pl.semaphore_wait(barrier, n_chips + max(n_grp - 1, 0))

    locals_ = [
        pltpu.make_async_copy(srcs[i], outs[i].at[chip, core], local_sems.at[i]) for i in range(n_in)
    ]
    for copy in locals_:
        copy.start()

    def remote(i, k):
        other = lax.rem(chip + k, n_chips)
        return pltpu.make_async_remote_copy(
            src_ref=srcs[i],
            dst_ref=outs[i].at[chip, core],
            send_sem=send_sems.at[i, k],
            recv_sem=recv_sems.at[i, chip],
            device_id=(grp, other * 2 + core),
            device_id_type=mesh_id,
        )

    def send(k, carry):
        for i in range(n_in):
            remote(i, k).start()
        return carry

    lax.fori_loop(1, n_chips, send, 0)

    if n_grp:
        quarter = summand.shape[1] // n_grp

        def scatter(j):
            target = lax.rem(grp + j, n_grp)
            return pltpu.make_async_remote_copy(
                src_ref=summand.at[:, pl.ds(target * quarter, quarter)],
                dst_ref=parts_in.at[grp],
                send_sem=rs_send.at[j],
                recv_sem=rs_recv.at[grp],
                device_id=(target, me),
                device_id_type=mesh_id,
            )

        for j in range(1, n_grp):
            scatter(j).start()
        for j in range(1, n_grp):
            scatter(j).wait_send()
            source = lax.rem(grp + j, n_grp)
            pltpu.make_async_copy(parts_in.at[source], parts_in.at[source], rs_recv.at[source]).wait()
        mine = pl.ds(grp * quarter, quarter)
        total = summand[:, mine, :].astype(jnp.float32)
        for j in range(1, n_grp):
            total = total + parts_in[lax.rem(grp + j, n_grp)].astype(jnp.float32)
        summed[:, mine, :] = total.astype(summed.dtype)

        def spread(j):
            target = lax.rem(grp + j, n_grp)
            return pltpu.make_async_remote_copy(
                src_ref=summed.at[:, mine],
                dst_ref=summed.at[:, mine],
                send_sem=ag_send.at[j],
                recv_sem=ag_recv.at[grp],
                device_id=(target, me),
                device_id_type=mesh_id,
            )

        for j in range(1, n_grp):
            spread(j).start()

    def arrive(k, carry):
        other = lax.rem(chip + k, n_chips)
        for i in range(n_in):
            remote(i, k).wait_send()
            pltpu.make_async_copy(
                srcs[i], outs[i].at[other, core], recv_sems.at[i, other]
            ).wait()
        return carry

    lax.fori_loop(1, n_chips, arrive, 0)
    for copy in locals_:
        copy.wait()

    def forward(i, c):
        return pltpu.make_async_remote_copy(
            src_ref=outs[i].at[c, core],
            dst_ref=outs[i].at[c, core],
            send_sem=fwd_send.at[i, c],
            recv_sem=fwd_recv.at[i, c],
            device_id=(grp, sibling),
            device_id_type=mesh_id,
        )

    def push(c, carry):
        for i in range(n_in):
            forward(i, c).start()
        return carry

    lax.fori_loop(0, n_chips, push, 0)

    def land(c, carry):
        for i in range(n_in):
            forward(i, c).wait_send()
            pltpu.make_async_copy(
                outs[i].at[c, core], outs[i].at[c, 1 - core], fwd_recv.at[i, c]
            ).wait()
        return carry

    lax.fori_loop(0, n_chips, land, 0)

    if n_grp:
        for j in range(1, n_grp):
            spread(j).wait_send()
            source = lax.rem(grp + j, n_grp)
            rows = pl.ds(source * quarter, quarter)
            pltpu.make_async_copy(summed.at[:, rows], summed.at[:, rows], ag_recv.at[source]).wait()


def fetch_group(n_tok, collective_id, parts, after, summand=None):
    if summand is None:
        parts = list(lax.optimization_barrier((tuple(parts), after))[0])
    n_chips = n_tok // 2
    n_in = len(parts)
    n_grp = 0 if summand is None else lax.axis_size("grp")
    moved = 2 * n_tok * sum(p.size for p in parts) * parts[0].dtype.itemsize
    out_shape = [jax.ShapeDtypeStruct((n_chips, 2) + p.shape, p.dtype) for p in parts]
    out_specs = [pl.BlockSpec(memory_space=pl.ANY) for _ in parts]
    in_specs = [pl.BlockSpec(memory_space=pl.ANY)] * n_in
    operands = list(parts)
    scratch = [
        pltpu.SemaphoreType.DMA((n_in, n_chips)),
        pltpu.SemaphoreType.DMA((n_in, n_chips)),
        pltpu.SemaphoreType.DMA((n_in,)),
        pltpu.SemaphoreType.DMA((n_in, n_chips)),
        pltpu.SemaphoreType.DMA((n_in, n_chips)),
    ]
    if n_grp:
        requests, slots, width = summand.shape
        operands.append(summand)
        in_specs.append(pl.BlockSpec(memory_space=pltpu.VMEM))
        out_shape.append(jax.ShapeDtypeStruct(summand.shape, summand.dtype))
        out_specs.append(pl.BlockSpec(memory_space=pltpu.VMEM))
        scratch += [
            pltpu.VMEM((n_grp, requests, slots // n_grp, width), summand.dtype),
            pltpu.SemaphoreType.DMA((n_grp,)),
            pltpu.SemaphoreType.DMA((n_grp,)),
            pltpu.SemaphoreType.DMA((n_grp,)),
            pltpu.SemaphoreType.DMA((n_grp,)),
        ]
    results = pl.pallas_call(
        functools.partial(gather_kernel, n_chips, n_in, n_grp),
        out_shape=tuple(out_shape),
        in_specs=in_specs,
        out_specs=tuple(out_specs),
        scratch_shapes=scratch,
        compiler_params=pltpu.CompilerParams(collective_id=collective_id, has_side_effects=True),
        cost_estimate=pl.CostEstimate(flops=0, transcendentals=0, bytes_accessed=moved),
    )(*operands)
    gathered = [g.reshape((n_tok * g.shape[2],) + g.shape[3:]) for g in results[:n_in]]
    if n_grp:
        return gathered, results[n_in]
    return gathered

def layer_sum(summand, base_full):
    return lax.psum(summand.astype(jnp.bfloat16), "grp").astype(jnp.float32) + base_full


def normed_rows(stream, gain_vec):
    scaled = rms_scale(stream, gain_vec)
    return scaled.reshape(-1, scaled.shape[-1])


def shards(
    hidden,
    draft_qkv,
    self_cache,
    cross_cache,
    parents,
    counts,
    self_len,
    enc_len,
    buckets,
    bias_table,
    gain_cross,
    gain_ffn,
    gain_next,
    w_out_self,
    w_query_cross,
    w_out_cross,
    w_gate,
    w_up,
    w_down,
    w_qkv,
):
    requests, share_rows, model_width = hidden.shape
    draft_slots = draft_qkv.shape[2]
    head_width = draft_qkv.shape[3]
    self_context = draft_attention(
        draft_qkv, self_cache, parents, counts, self_len, buckets, bias_table
    )
    (w_out_self_t,) = fetch_group(lax.axis_size("tok"), 3, (w_out_self.T,), self_context)
    partial_value = jnp.einsum(
        "rk,ok->ro", self_context, w_out_self_t, preferred_element_type=jnp.float32
    )
    partial_value = partial_value.reshape(requests, draft_slots, model_width)
    own_rows = hidden.astype(jnp.float32)
    offset = lax.axis_index("grp") * share_rows
    placed = lax.dynamic_update_slice(
        jnp.zeros((requests, draft_slots, model_width), jnp.float32), own_rows, (0, offset, 0)
    )
    summand = partial_value + placed
    n_tok = lax.axis_size("tok")
    (w_query_full, w_out_cross_t, w_gate_full), summed = fetch_group(
        n_tok, 0, (w_query_cross, w_out_cross.T, w_gate), None, summand.astype(jnp.bfloat16)
    )
    stream_one = summed.astype(jnp.float32)
    normed_one = normed_rows(stream_one, gain_cross)
    cross_query = jnp.dot(normed_one, w_query_full, preferred_element_type=jnp.float32)
    cross_query = cross_query.astype(jnp.bfloat16).reshape(requests, draft_slots, head_width)
    cross_context = cross_attention(cross_query, cross_cache, enc_len)
    partial_value = jnp.einsum(
        "rk,ok->ro", cross_context, w_out_cross_t, preferred_element_type=jnp.float32
    )
    (w_up_full, w_down_t), summed = fetch_group(
        n_tok, 1, (w_up, w_down.T), None,
        partial_value.reshape(requests, draft_slots, model_width).astype(jnp.bfloat16),
    )
    stream_two = summed.astype(jnp.float32) + stream_one
    normed_two = normed_rows(stream_two, gain_ffn)
    gate_part = jnp.dot(normed_two, w_gate_full, preferred_element_type=jnp.float32)
    up_part = jnp.dot(normed_two, w_up_full, preferred_element_type=jnp.float32)
    gated = (jax.nn.gelu(gate_part, approximate=True) * up_part).astype(jnp.bfloat16)
    partial_value = jnp.einsum("rk,ok->ro", gated, w_down_t, preferred_element_type=jnp.float32)
    (w_qkv_full,), summed = fetch_group(
        n_tok, 2, (w_qkv.reshape(w_qkv.shape[0], -1),), None,
        partial_value.reshape(requests, draft_slots, model_width).astype(jnp.bfloat16),
    )
    stream_three = summed.astype(jnp.float32) + stream_two
    normed_three = normed_rows(stream_three, gain_next)
    projected = jnp.dot(
        normed_three,
        w_qkv_full.reshape(w_qkv_full.shape[0], -1),
        preferred_element_type=jnp.float32,
    )
    projected = projected.astype(jnp.bfloat16).reshape(requests, draft_slots, 3, head_width)
    next_qkv = jnp.transpose(projected, (2, 0, 1, 3))
    out_hidden = lax.dynamic_slice_in_dim(stream_three, offset, share_rows, 1).astype(jnp.bfloat16)
    return (out_hidden, next_qkv)


def solution(mesh):
    in_specs = (
        P("tok", "grp", None),
        P(None, "tok", None, "grp"),
        P("tok", None, None, "grp"),
        P("tok", None, None, "grp"),
        P("tok", None),
        P("tok"),
        P("tok"),
        P("tok"),
        P("tok", None, None),
        P(None, "grp"),
        P(),
        P(),
        P(),
        P("grp", "tok"),
        P("tok", "grp"),
        P("grp", "tok"),
        P("tok", "grp"),
        P("tok", "grp"),
        P("grp", "tok"),
        P("tok", None, "grp"),
    )
    out_specs = (P("tok", "grp", None), P(None, "tok", None, "grp"))
    return jax.shard_map(shards, mesh=mesh, in_specs=in_specs, out_specs=out_specs, check_vma=False)
```

```python
import functools

import jax
import jax.numpy as jnp
from jax import lax
from jax.experimental import pallas as pl
from jax.experimental.pallas import tpu as pltpu
from jax.sharding import PartitionSpec as P

DH = 64


def ancestor_table(parent_ids):
    count_slots = parent_ids.shape[0]
    slot_ids = jnp.arange(count_slots, dtype=jnp.int32)
    ancestors = jnp.eye(count_slots, dtype=jnp.float32) + (
        parent_ids[:, None] == slot_ids[None, :]
    ).astype(jnp.float32)
    for repeat in range(max(1, count_slots.bit_length())):
        ancestors = jnp.minimum(jnp.dot(ancestors, ancestors, precision=lax.Precision.HIGHEST), 1.0)
    return ancestors


def rms_scale(stream, gain_vec):
    mean_square = jnp.mean(stream * stream, axis=-1, keepdims=True)
    return (stream * lax.rsqrt(mean_square + 1e-06) * gain_vec).astype(jnp.bfloat16)


def draft_attention(projected, cached, parent_ids, draft_count, length, bucket_ids, bias_table):
    requests, draft_slots, head_width = (projected.shape[1], projected.shape[2], projected.shape[3])
    local_heads = bias_table.shape[1]
    head_size = head_width // local_heads
    queries = projected[0].reshape(requests, draft_slots, local_heads, head_size)
    draft_keys = projected[1].reshape(requests, draft_slots, local_heads, head_size)
    draft_values = projected[2].reshape(requests, draft_slots, local_heads, head_size)
    cache_keys = cached[:, 0].reshape(requests, -1, local_heads, head_size)
    cache_values = cached[:, 1].reshape(requests, -1, local_heads, head_size)
    cache_scores = jnp.einsum(
        "rihd,rphd->rhip", queries, cache_keys, preferred_element_type=jnp.float32
    )
    cache_scores = cache_scores + bias_table[-1][None, :, None, None]
    cache_live = jnp.arange(cache_keys.shape[1], dtype=jnp.int32)[None, :] < length[:, None]
    cache_scores = jnp.where(cache_live[:, None, None, :], cache_scores, -1e30)
    onehot = (bucket_ids[..., None] == jnp.arange(bias_table.shape[0], dtype=jnp.int32)).astype(
        jnp.float32
    )
    draft_bias = jnp.einsum("rijb,bh->rhij", onehot, bias_table, precision=lax.Precision.HIGHEST)
    draft_scores = (
        jnp.einsum("rihd,rjhd->rhij", queries, draft_keys, preferred_element_type=jnp.float32)
        + draft_bias
    )
    ancestors = jax.vmap(ancestor_table)(parent_ids)
    draft_live = (ancestors > 0.5) & (
        jnp.arange(draft_slots, dtype=jnp.int32)[None, None, :] < draft_count[:, None, None]
    )
    draft_scores = jnp.where(draft_live[:, None], draft_scores, -1e30)
    highest = jnp.maximum(cache_scores.max(-1, keepdims=True), draft_scores.max(-1, keepdims=True))
    exp_cache = jnp.exp(cache_scores - highest)
    exp_draft = jnp.exp(draft_scores - highest)
    denominator = exp_cache.sum(-1, keepdims=True) + exp_draft.sum(-1, keepdims=True)
    weights_cache = (exp_cache / denominator).astype(jnp.bfloat16)
    weights_draft = (exp_draft / denominator).astype(jnp.bfloat16)
    attended = jnp.einsum(
        "rhip,rphd->rihd", weights_cache, cache_values, preferred_element_type=jnp.float32
    )
    attended = attended + jnp.einsum(
        "rhij,rjhd->rihd", weights_draft, draft_values, preferred_element_type=jnp.float32
    )
    return attended.astype(jnp.bfloat16).reshape(requests * draft_slots, head_width)


def cross_attention(query_rows, cached, length):
    requests, draft_slots, head_width = query_rows.shape
    local_heads = head_width // DH
    queries = query_rows.reshape(requests, draft_slots, local_heads, DH)
    enc_keys = cached[:, 0].reshape(requests, -1, local_heads, DH)
    enc_values = cached[:, 1].reshape(requests, -1, local_heads, DH)
    scores = jnp.einsum("rihd,rphd->rhip", queries, enc_keys, preferred_element_type=jnp.float32)
    live = jnp.arange(enc_keys.shape[1], dtype=jnp.int32)[None, :] < length[:, None]
    scores = jnp.where(live[:, None, None, :], scores, -1e30)
    highest = scores.max(-1, keepdims=True)
    exp_scores = jnp.exp(scores - highest)
    weights = (exp_scores / exp_scores.sum(-1, keepdims=True)).astype(jnp.bfloat16)
    attended = jnp.einsum(
        "rhip,rphd->rihd", weights, enc_values, preferred_element_type=jnp.float32
    )
    return attended.astype(jnp.bfloat16).reshape(requests * draft_slots, head_width)


def cross_kernel(len_ref, q_ref, kv_ref, o_ref):
    length = len_ref[pl.program_id(0)]
    q = q_ref[0]
    keys = kv_ref[0, 0]
    values = kv_ref[0, 1]
    live = lax.broadcasted_iota(jnp.int32, (q.shape[0], keys.shape[0]), 1) < length
    for h in range(q.shape[1] // DH):
        cols = slice(h * DH, (h + 1) * DH)
        scores = lax.dot_general(
            q[:, cols], keys[:, cols], (((1,), (1,)), ((), ())), preferred_element_type=jnp.float32
        )
        scores = jnp.where(live, scores, -1e30)
        exp_scores = jnp.exp(scores - scores.max(-1, keepdims=True))
        weights = (exp_scores / exp_scores.sum(-1, keepdims=True)).astype(jnp.bfloat16)
        o_ref[0, :, cols] = jnp.dot(
            weights, values[:, cols], preferred_element_type=jnp.float32
        ).astype(o_ref.dtype)


def cross_attention_kernel(query_rows, cached, length):
    requests, draft_slots, head_width = query_rows.shape
    positions = cached.shape[2]
    attended = pl.pallas_call(
        cross_kernel,
        out_shape=jax.ShapeDtypeStruct(query_rows.shape, jnp.bfloat16),
        grid_spec=pltpu.PrefetchScalarGridSpec(
            num_scalar_prefetch=1,
            grid=(requests,),
            in_specs=[
                pl.BlockSpec((1, draft_slots, head_width), lambda r, lens: (r, 0, 0)),
                pl.BlockSpec((1, 2, positions, head_width), lambda r, lens: (r, 0, 0, 0)),
            ],
            out_specs=pl.BlockSpec((1, draft_slots, head_width), lambda r, lens: (r, 0, 0)),
        ),
        cost_estimate=pl.CostEstimate(
            flops=4 * requests * draft_slots * positions * head_width,
            transcendentals=requests * draft_slots * positions * (head_width // DH),
            bytes_accessed=2 * cached.size + 4 * query_rows.size,
        ),
    )(length, query_rows, cached)
    return attended.reshape(requests * draft_slots, head_width)


def gather_kernel(n_chips, n_in, n_grp, *refs):
    srcs = refs[:n_in]
    if n_grp:
        summand = refs[n_in]
        outs = refs[n_in + 1:2 * n_in + 1]
        summed = refs[2 * n_in + 1]
        rest = refs[2 * n_in + 2:]
        send_sems, recv_sems, local_sems, fwd_send, fwd_recv, parts_in, rs_send, rs_recv, ag_send, ag_recv = rest
    else:
        outs = refs[n_in:2 * n_in]
        send_sems, recv_sems, local_sems, fwd_send, fwd_recv = refs[2 * n_in:]
    grp = lax.axis_index("grp")
    me = lax.axis_index("tok")
    chip = me // 2
    core = me % 2
    sibling = chip * 2 + (1 - core)
    mesh_id = pl.DeviceIdType.MESH

    barrier = pltpu.get_barrier_semaphore()
    for k in range(1, n_chips):
        peer = lax.rem(chip + k, n_chips) * 2 + core
        pl.semaphore_signal(barrier, inc=1, device_id=(grp, peer), device_id_type=mesh_id)
    pl.semaphore_signal(barrier, inc=1, device_id=(grp, sibling), device_id_type=mesh_id)
    for j in range(1, max(n_grp, 1)):
        pl.semaphore_signal(
            barrier, inc=1, device_id=(lax.rem(grp + j, n_grp), me), device_id_type=mesh_id
        )
    pl.semaphore_wait(barrier, n_chips + max(n_grp - 1, 0))

    locals_ = [
        pltpu.make_async_copy(srcs[i], outs[i].at[chip, core], local_sems.at[i]) for i in range(n_in)
    ]
    for copy in locals_:
        copy.start()

    def remote(i, k):
        other = lax.rem(chip + k, n_chips)
        return pltpu.make_async_remote_copy(
            src_ref=srcs[i],
            dst_ref=outs[i].at[chip, core],
            send_sem=send_sems.at[i, k],
            recv_sem=recv_sems.at[i, chip],
            device_id=(grp, other * 2 + core),
            device_id_type=mesh_id,
        )

    def send(k, carry):
        for i in range(n_in):
            remote(i, k).start()
        return carry

    lax.fori_loop(1, n_chips, send, 0)

    if n_grp:
        quarter = summand.shape[1] // n_grp

        def scatter(j):
            target = lax.rem(grp + j, n_grp)
            return pltpu.make_async_remote_copy(
                src_ref=summand.at[:, pl.ds(target * quarter, quarter)],
                dst_ref=parts_in.at[grp],
                send_sem=rs_send.at[j],
                recv_sem=rs_recv.at[grp],
                device_id=(target, me),
                device_id_type=mesh_id,
            )

        for j in range(1, n_grp):
            scatter(j).start()
        for j in range(1, n_grp):
            scatter(j).wait_send()
            source = lax.rem(grp + j, n_grp)
            pltpu.make_async_copy(parts_in.at[source], parts_in.at[source], rs_recv.at[source]).wait()
        mine = pl.ds(grp * quarter, quarter)
        total = summand[:, mine, :].astype(jnp.float32)
        for j in range(1, n_grp):
            total = total + parts_in[lax.rem(grp + j, n_grp)].astype(jnp.float32)
        summed[:, mine, :] = total.astype(summed.dtype)

        def spread(j):
            target = lax.rem(grp + j, n_grp)
            return pltpu.make_async_remote_copy(
                src_ref=summed.at[:, mine],
                dst_ref=summed.at[:, mine],
                send_sem=ag_send.at[j],
                recv_sem=ag_recv.at[grp],
                device_id=(target, me),
                device_id_type=mesh_id,
            )

        for j in range(1, n_grp):
            spread(j).start()

    def arrive(k, carry):
        other = lax.rem(chip + k, n_chips)
        for i in range(n_in):
            remote(i, k).wait_send()
            pltpu.make_async_copy(
                srcs[i], outs[i].at[other, core], recv_sems.at[i, other]
            ).wait()
        return carry

    lax.fori_loop(1, n_chips, arrive, 0)
    for copy in locals_:
        copy.wait()

    def forward(i, c):
        return pltpu.make_async_remote_copy(
            src_ref=outs[i].at[c, core],
            dst_ref=outs[i].at[c, core],
            send_sem=fwd_send.at[i, c],
            recv_sem=fwd_recv.at[i, c],
            device_id=(grp, sibling),
            device_id_type=mesh_id,
        )

    def push(c, carry):
        for i in range(n_in):
            forward(i, c).start()
        return carry

    lax.fori_loop(0, n_chips, push, 0)

    def land(c, carry):
        for i in range(n_in):
            forward(i, c).wait_send()
            pltpu.make_async_copy(
                outs[i].at[c, core], outs[i].at[c, 1 - core], fwd_recv.at[i, c]
            ).wait()
        return carry

    lax.fori_loop(0, n_chips, land, 0)

    if n_grp:
        for j in range(1, n_grp):
            spread(j).wait_send()
            source = lax.rem(grp + j, n_grp)
            rows = pl.ds(source * quarter, quarter)
            pltpu.make_async_copy(summed.at[:, rows], summed.at[:, rows], ag_recv.at[source]).wait()


def fetch_group(n_tok, collective_id, parts, after, summand=None):
    if summand is None:
        parts = list(lax.optimization_barrier((tuple(parts), after))[0])
    n_chips = n_tok // 2
    n_in = len(parts)
    n_grp = 0 if summand is None else lax.axis_size("grp")
    moved = 2 * n_tok * sum(p.size for p in parts) * parts[0].dtype.itemsize
    out_shape = [jax.ShapeDtypeStruct((n_chips, 2) + p.shape, p.dtype) for p in parts]
    out_specs = [pl.BlockSpec(memory_space=pl.ANY) for _ in parts]
    in_specs = [pl.BlockSpec(memory_space=pl.ANY)] * n_in
    operands = list(parts)
    scratch = [
        pltpu.SemaphoreType.DMA((n_in, n_chips)),
        pltpu.SemaphoreType.DMA((n_in, n_chips)),
        pltpu.SemaphoreType.DMA((n_in,)),
        pltpu.SemaphoreType.DMA((n_in, n_chips)),
        pltpu.SemaphoreType.DMA((n_in, n_chips)),
    ]
    if n_grp:
        requests, slots, width = summand.shape
        operands.append(summand)
        in_specs.append(pl.BlockSpec(memory_space=pltpu.VMEM))
        out_shape.append(jax.ShapeDtypeStruct(summand.shape, summand.dtype))
        out_specs.append(pl.BlockSpec(memory_space=pltpu.VMEM))
        scratch += [
            pltpu.VMEM((n_grp, requests, slots // n_grp, width), summand.dtype),
            pltpu.SemaphoreType.DMA((n_grp,)),
            pltpu.SemaphoreType.DMA((n_grp,)),
            pltpu.SemaphoreType.DMA((n_grp,)),
            pltpu.SemaphoreType.DMA((n_grp,)),
        ]
    results = pl.pallas_call(
        functools.partial(gather_kernel, n_chips, n_in, n_grp),
        out_shape=tuple(out_shape),
        in_specs=in_specs,
        out_specs=tuple(out_specs),
        scratch_shapes=scratch,
        compiler_params=pltpu.CompilerParams(collective_id=collective_id, has_side_effects=True),
        cost_estimate=pl.CostEstimate(flops=0, transcendentals=0, bytes_accessed=moved),
    )(*operands)
    gathered = [g.reshape((n_tok * g.shape[2],) + g.shape[3:]) for g in results[:n_in]]
    if n_grp:
        return gathered, results[n_in]
    return gathered

def layer_sum(summand, base_full):
    return lax.psum(summand.astype(jnp.bfloat16), "grp").astype(jnp.float32) + base_full


def normed_rows(stream, gain_vec):
    scaled = rms_scale(stream, gain_vec)
    return scaled.reshape(-1, scaled.shape[-1])


def shards(
    hidden,
    draft_qkv,
    self_cache,
    cross_cache,
    parents,
    counts,
    self_len,
    enc_len,
    buckets,
    bias_table,
    gain_cross,
    gain_ffn,
    gain_next,
    w_out_self,
    w_query_cross,
    w_out_cross,
    w_gate,
    w_up,
    w_down,
    w_qkv,
):
    requests, share_rows, model_width = hidden.shape
    draft_slots = draft_qkv.shape[2]
    head_width = draft_qkv.shape[3]
    self_context = draft_attention(
        draft_qkv, self_cache, parents, counts, self_len, buckets, bias_table
    )
    (w_out_self_t,) = fetch_group(lax.axis_size("tok"), 3, (w_out_self.T,), self_context)
    partial_value = jnp.einsum(
        "rk,ok->ro", self_context, w_out_self_t, preferred_element_type=jnp.float32
    )
    partial_value = partial_value.reshape(requests, draft_slots, model_width)
    own_rows = hidden.astype(jnp.float32)
    offset = lax.axis_index("grp") * share_rows
    placed = lax.dynamic_update_slice(
        jnp.zeros((requests, draft_slots, model_width), jnp.float32), own_rows, (0, offset, 0)
    )
    summand = partial_value + placed
    n_tok = lax.axis_size("tok")
    (w_query_full, w_out_cross_t, w_gate_full), summed = fetch_group(
        n_tok, 0, (w_query_cross, w_out_cross.T, w_gate), None, summand.astype(jnp.bfloat16)
    )
    stream_one = summed.astype(jnp.float32)
    normed_one = normed_rows(stream_one, gain_cross)
    cross_query = jnp.dot(normed_one, w_query_full, preferred_element_type=jnp.float32)
    cross_query = cross_query.astype(jnp.bfloat16).reshape(requests, draft_slots, head_width)
    cross_context = cross_attention_kernel(cross_query, cross_cache, enc_len)
    partial_value = jnp.einsum(
        "rk,ok->ro", cross_context, w_out_cross_t, preferred_element_type=jnp.float32
    )
    (w_up_full, w_down_t), summed = fetch_group(
        n_tok, 1, (w_up, w_down.T), None,
        partial_value.reshape(requests, draft_slots, model_width).astype(jnp.bfloat16),
    )
    stream_two = summed.astype(jnp.float32) + stream_one
    normed_two = normed_rows(stream_two, gain_ffn)
    gate_part = jnp.dot(normed_two, w_gate_full, preferred_element_type=jnp.float32)
    up_part = jnp.dot(normed_two, w_up_full, preferred_element_type=jnp.float32)
    gated = (jax.nn.gelu(gate_part, approximate=True) * up_part).astype(jnp.bfloat16)
    partial_value = jnp.einsum("rk,ok->ro", gated, w_down_t, preferred_element_type=jnp.float32)
    (w_qkv_full,), summed = fetch_group(
        n_tok, 2, (w_qkv.reshape(w_qkv.shape[0], -1),), None,
        partial_value.reshape(requests, draft_slots, model_width).astype(jnp.bfloat16),
    )
    stream_three = summed.astype(jnp.float32) + stream_two
    normed_three = normed_rows(stream_three, gain_next)
    projected = jnp.dot(
        normed_three,
        w_qkv_full.reshape(w_qkv_full.shape[0], -1),
        preferred_element_type=jnp.float32,
    )
    projected = projected.astype(jnp.bfloat16).reshape(requests, draft_slots, 3, head_width)
    next_qkv = jnp.transpose(projected, (2, 0, 1, 3))
    out_hidden = lax.dynamic_slice_in_dim(stream_three, offset, share_rows, 1).astype(jnp.bfloat16)
    return (out_hidden, next_qkv)


def solution(mesh):
    in_specs = (
        P("tok", "grp", None),
        P(None, "tok", None, "grp"),
        P("tok", None, None, "grp"),
        P("tok", None, None, "grp"),
        P("tok", None),
        P("tok"),
        P("tok"),
        P("tok"),
        P("tok", None, None),
        P(None, "grp"),
        P(),
        P(),
        P(),
        P("grp", "tok"),
        P("tok", "grp"),
        P("grp", "tok"),
        P("tok", "grp"),
        P("tok", "grp"),
        P("grp", "tok"),
        P("tok", None, "grp"),
    )
    out_specs = (P("tok", "grp", None), P(None, "tok", None, "grp"))
    return jax.shard_map(shards, mesh=mesh, in_specs=in_specs, out_specs=out_specs, check_vma=False)
```

```python
import functools

import jax
import jax.numpy as jnp
from jax import lax
from jax.experimental import pallas as pl
from jax.experimental.pallas import tpu as pltpu
from jax.sharding import PartitionSpec as P

DH = 64


def ancestor_table(parent_ids):
    count_slots = parent_ids.shape[0]
    slot_ids = jnp.arange(count_slots, dtype=jnp.int32)
    ancestors = jnp.eye(count_slots, dtype=jnp.float32) + (
        parent_ids[:, None] == slot_ids[None, :]
    ).astype(jnp.float32)
    for repeat in range(max(1, count_slots.bit_length())):
        ancestors = jnp.minimum(jnp.dot(ancestors, ancestors, precision=lax.Precision.HIGHEST), 1.0)
    return ancestors


def rms_scale(stream, gain_vec):
    mean_square = jnp.mean(stream * stream, axis=-1, keepdims=True)
    return (stream * lax.rsqrt(mean_square + 1e-06) * gain_vec).astype(jnp.bfloat16)


def draft_attention(projected, cached, parent_ids, draft_count, length, bucket_ids, bias_table):
    requests, draft_slots, head_width = (projected.shape[1], projected.shape[2], projected.shape[3])
    local_heads = bias_table.shape[1]
    head_size = head_width // local_heads
    queries = projected[0].reshape(requests, draft_slots, local_heads, head_size)
    draft_keys = projected[1].reshape(requests, draft_slots, local_heads, head_size)
    draft_values = projected[2].reshape(requests, draft_slots, local_heads, head_size)
    cache_keys = cached[:, 0].reshape(requests, -1, local_heads, head_size)
    cache_values = cached[:, 1].reshape(requests, -1, local_heads, head_size)
    cache_scores = jnp.einsum(
        "rihd,rphd->rhip", queries, cache_keys, preferred_element_type=jnp.float32
    )
    cache_scores = cache_scores + bias_table[-1][None, :, None, None]
    cache_live = jnp.arange(cache_keys.shape[1], dtype=jnp.int32)[None, :] < length[:, None]
    cache_scores = jnp.where(cache_live[:, None, None, :], cache_scores, -1e30)
    onehot = (bucket_ids[..., None] == jnp.arange(bias_table.shape[0], dtype=jnp.int32)).astype(
        jnp.float32
    )
    draft_bias = jnp.einsum("rijb,bh->rhij", onehot, bias_table, precision=lax.Precision.HIGHEST)
    draft_scores = (
        jnp.einsum("rihd,rjhd->rhij", queries, draft_keys, preferred_element_type=jnp.float32)
        + draft_bias
    )
    ancestors = jax.vmap(ancestor_table)(parent_ids)
    draft_live = (ancestors > 0.5) & (
        jnp.arange(draft_slots, dtype=jnp.int32)[None, None, :] < draft_count[:, None, None]
    )
    draft_scores = jnp.where(draft_live[:, None], draft_scores, -1e30)
    highest = jnp.maximum(cache_scores.max(-1, keepdims=True), draft_scores.max(-1, keepdims=True))
    exp_cache = jnp.exp(cache_scores - highest)
    exp_draft = jnp.exp(draft_scores - highest)
    denominator = exp_cache.sum(-1, keepdims=True) + exp_draft.sum(-1, keepdims=True)
    weights_cache = (exp_cache / denominator).astype(jnp.bfloat16)
    weights_draft = (exp_draft / denominator).astype(jnp.bfloat16)
    attended = jnp.einsum(
        "rhip,rphd->rihd", weights_cache, cache_values, preferred_element_type=jnp.float32
    )
    attended = attended + jnp.einsum(
        "rhij,rjhd->rihd", weights_draft, draft_values, preferred_element_type=jnp.float32
    )
    return attended.astype(jnp.bfloat16).reshape(requests * draft_slots, head_width)


def cross_attention(query_rows, cached, length):
    requests, draft_slots, head_width = query_rows.shape
    local_heads = head_width // DH
    queries = query_rows.reshape(requests, draft_slots, local_heads, DH)
    enc_keys = cached[:, 0].reshape(requests, -1, local_heads, DH)
    enc_values = cached[:, 1].reshape(requests, -1, local_heads, DH)
    scores = jnp.einsum("rihd,rphd->rhip", queries, enc_keys, preferred_element_type=jnp.float32)
    live = jnp.arange(enc_keys.shape[1], dtype=jnp.int32)[None, :] < length[:, None]
    scores = jnp.where(live[:, None, None, :], scores, -1e30)
    highest = scores.max(-1, keepdims=True)
    exp_scores = jnp.exp(scores - highest)
    weights = (exp_scores / exp_scores.sum(-1, keepdims=True)).astype(jnp.bfloat16)
    attended = jnp.einsum(
        "rhip,rphd->rihd", weights, enc_values, preferred_element_type=jnp.float32
    )
    return attended.astype(jnp.bfloat16).reshape(requests * draft_slots, head_width)


def gather_kernel(n_chips, n_in, n_grp, *refs):
    srcs = refs[:n_in]
    if n_grp:
        summand = refs[n_in]
        outs = refs[n_in + 1:2 * n_in + 1]
        summed = refs[2 * n_in + 1]
        rest = refs[2 * n_in + 2:]
        send_sems, recv_sems, local_sems, fwd_send, fwd_recv, parts_in, rs_send, rs_recv, ag_send, ag_recv = rest
    else:
        outs = refs[n_in:2 * n_in]
        send_sems, recv_sems, local_sems, fwd_send, fwd_recv = refs[2 * n_in:]
    grp = lax.axis_index("grp")
    me = lax.axis_index("tok")
    chip = me // 2
    core = me % 2
    sibling = chip * 2 + (1 - core)
    mesh_id = pl.DeviceIdType.MESH

    barrier = pltpu.get_barrier_semaphore()
    for k in range(1, n_chips):
        peer = lax.rem(chip + k, n_chips) * 2 + core
        pl.semaphore_signal(barrier, inc=1, device_id=(grp, peer), device_id_type=mesh_id)
    pl.semaphore_signal(barrier, inc=1, device_id=(grp, sibling), device_id_type=mesh_id)
    for j in range(1, max(n_grp, 1)):
        pl.semaphore_signal(
            barrier, inc=1, device_id=(lax.rem(grp + j, n_grp), me), device_id_type=mesh_id
        )
    pl.semaphore_wait(barrier, n_chips + max(n_grp - 1, 0))

    locals_ = [
        pltpu.make_async_copy(srcs[i], outs[i].at[chip, core], local_sems.at[i]) for i in range(n_in)
    ]
    for copy in locals_:
        copy.start()

    def remote(i, k):
        other = lax.rem(chip + k, n_chips)
        return pltpu.make_async_remote_copy(
            src_ref=srcs[i],
            dst_ref=outs[i].at[chip, core],
            send_sem=send_sems.at[i, k],
            recv_sem=recv_sems.at[i, chip],
            device_id=(grp, other * 2 + core),
            device_id_type=mesh_id,
        )

    def send(k, carry):
        for i in range(n_in):
            remote(i, k).start()
        return carry

    lax.fori_loop(1, n_chips, send, 0)

    if n_grp:
        quarter = summand.shape[1] // n_grp

        def scatter(j):
            target = lax.rem(grp + j, n_grp)
            return pltpu.make_async_remote_copy(
                src_ref=summand.at[:, pl.ds(target * quarter, quarter)],
                dst_ref=parts_in.at[grp],
                send_sem=rs_send.at[j],
                recv_sem=rs_recv.at[grp],
                device_id=(target, me),
                device_id_type=mesh_id,
            )

        for j in range(1, n_grp):
            scatter(j).start()
        for j in range(1, n_grp):
            scatter(j).wait_send()
            source = lax.rem(grp + j, n_grp)
            pltpu.make_async_copy(parts_in.at[source], parts_in.at[source], rs_recv.at[source]).wait()
        mine = pl.ds(grp * quarter, quarter)
        total = summand[:, mine, :].astype(jnp.float32)
        for j in range(1, n_grp):
            total = total + parts_in[lax.rem(grp + j, n_grp)].astype(jnp.float32)
        summed[:, mine, :] = total.astype(summed.dtype)

        def spread(j):
            target = lax.rem(grp + j, n_grp)
            return pltpu.make_async_remote_copy(
                src_ref=summed.at[:, mine],
                dst_ref=summed.at[:, mine],
                send_sem=ag_send.at[j],
                recv_sem=ag_recv.at[grp],
                device_id=(target, me),
                device_id_type=mesh_id,
            )

        for j in range(1, n_grp):
            spread(j).start()

    def forward(i, c):
        return pltpu.make_async_remote_copy(
            src_ref=outs[i].at[c, core],
            dst_ref=outs[i].at[c, core],
            send_sem=fwd_send.at[i, c],
            recv_sem=fwd_recv.at[i, c],
            device_id=(grp, sibling),
            device_id_type=mesh_id,
        )

    for i in range(n_in):
        locals_[i].wait()
        forward(i, chip).start()

    def arrive(k, carry):
        other = lax.rem(chip + k, n_chips)
        for i in range(n_in):
            pltpu.make_async_copy(
                srcs[i], outs[i].at[other, core], recv_sems.at[i, other]
            ).wait()
            forward(i, other).start()
        for i in range(n_in):
            remote(i, k).wait_send()
        return carry

    lax.fori_loop(1, n_chips, arrive, 0)

    def land(c, carry):
        for i in range(n_in):
            forward(i, c).wait_send()
            pltpu.make_async_copy(
                outs[i].at[c, core], outs[i].at[c, 1 - core], fwd_recv.at[i, c]
            ).wait()
        return carry

    lax.fori_loop(0, n_chips, land, 0)

    if n_grp:
        for j in range(1, n_grp):
            spread(j).wait_send()
            source = lax.rem(grp + j, n_grp)
            rows = pl.ds(source * quarter, quarter)
            pltpu.make_async_copy(summed.at[:, rows], summed.at[:, rows], ag_recv.at[source]).wait()


def fetch_group(n_tok, collective_id, parts, after, summand=None):
    if summand is None:
        parts = list(lax.optimization_barrier((tuple(parts), after))[0])
    n_chips = n_tok // 2
    n_in = len(parts)
    n_grp = 0 if summand is None else lax.axis_size("grp")
    moved = 2 * n_tok * sum(p.size for p in parts) * parts[0].dtype.itemsize
    out_shape = [jax.ShapeDtypeStruct((n_chips, 2) + p.shape, p.dtype) for p in parts]
    out_specs = [pl.BlockSpec(memory_space=pl.ANY) for _ in parts]
    in_specs = [pl.BlockSpec(memory_space=pl.ANY)] * n_in
    operands = list(parts)
    scratch = [
        pltpu.SemaphoreType.DMA((n_in, n_chips)),
        pltpu.SemaphoreType.DMA((n_in, n_chips)),
        pltpu.SemaphoreType.DMA((n_in,)),
        pltpu.SemaphoreType.DMA((n_in, n_chips)),
        pltpu.SemaphoreType.DMA((n_in, n_chips)),
    ]
    if n_grp:
        requests, slots, width = summand.shape
        operands.append(summand)
        in_specs.append(pl.BlockSpec(memory_space=pltpu.VMEM))
        out_shape.append(jax.ShapeDtypeStruct(summand.shape, summand.dtype))
        out_specs.append(pl.BlockSpec(memory_space=pltpu.VMEM))
        scratch += [
            pltpu.VMEM((n_grp, requests, slots // n_grp, width), summand.dtype),
            pltpu.SemaphoreType.DMA((n_grp,)),
            pltpu.SemaphoreType.DMA((n_grp,)),
            pltpu.SemaphoreType.DMA((n_grp,)),
            pltpu.SemaphoreType.DMA((n_grp,)),
        ]
    results = pl.pallas_call(
        functools.partial(gather_kernel, n_chips, n_in, n_grp),
        out_shape=tuple(out_shape),
        in_specs=in_specs,
        out_specs=tuple(out_specs),
        scratch_shapes=scratch,
        compiler_params=pltpu.CompilerParams(collective_id=collective_id, has_side_effects=True),
        cost_estimate=pl.CostEstimate(flops=0, transcendentals=0, bytes_accessed=moved),
    )(*operands)
    gathered = [g.reshape((n_tok * g.shape[2],) + g.shape[3:]) for g in results[:n_in]]
    if n_grp:
        return gathered, results[n_in]
    return gathered

def layer_sum(summand, base_full):
    return lax.psum(summand.astype(jnp.bfloat16), "grp").astype(jnp.float32) + base_full


def normed_rows(stream, gain_vec):
    scaled = rms_scale(stream, gain_vec)
    return scaled.reshape(-1, scaled.shape[-1])


def shards(
    hidden,
    draft_qkv,
    self_cache,
    cross_cache,
    parents,
    counts,
    self_len,
    enc_len,
    buckets,
    bias_table,
    gain_cross,
    gain_ffn,
    gain_next,
    w_out_self,
    w_query_cross,
    w_out_cross,
    w_gate,
    w_up,
    w_down,
    w_qkv,
):
    requests, share_rows, model_width = hidden.shape
    draft_slots = draft_qkv.shape[2]
    head_width = draft_qkv.shape[3]
    self_context = draft_attention(
        draft_qkv, self_cache, parents, counts, self_len, buckets, bias_table
    )
    (w_out_self_t,) = fetch_group(lax.axis_size("tok"), 3, (w_out_self.T,), self_context)
    partial_value = jnp.einsum(
        "rk,ok->ro", self_context, w_out_self_t, preferred_element_type=jnp.float32
    )
    partial_value = partial_value.reshape(requests, draft_slots, model_width)
    own_rows = hidden.astype(jnp.float32)
    offset = lax.axis_index("grp") * share_rows
    placed = lax.dynamic_update_slice(
        jnp.zeros((requests, draft_slots, model_width), jnp.float32), own_rows, (0, offset, 0)
    )
    summand = partial_value + placed
    n_tok = lax.axis_size("tok")
    (w_query_full, w_out_cross_t, w_gate_full), summed = fetch_group(
        n_tok, 0, (w_query_cross, w_out_cross.T, w_gate), None, summand.astype(jnp.bfloat16)
    )
    stream_one = summed.astype(jnp.float32)
    normed_one = normed_rows(stream_one, gain_cross)
    cross_query = jnp.dot(normed_one, w_query_full, preferred_element_type=jnp.float32)
    cross_query = cross_query.astype(jnp.bfloat16).reshape(requests, draft_slots, head_width)
    cross_context = cross_attention(cross_query, cross_cache, enc_len)
    partial_value = jnp.einsum(
        "rk,ok->ro", cross_context, w_out_cross_t, preferred_element_type=jnp.float32
    )
    (w_up_full, w_down_t), summed = fetch_group(
        n_tok, 1, (w_up, w_down.T), None,
        partial_value.reshape(requests, draft_slots, model_width).astype(jnp.bfloat16),
    )
    stream_two = summed.astype(jnp.float32) + stream_one
    normed_two = normed_rows(stream_two, gain_ffn)
    gate_part = jnp.dot(normed_two, w_gate_full, preferred_element_type=jnp.float32)
    up_part = jnp.dot(normed_two, w_up_full, preferred_element_type=jnp.float32)
    gated = (jax.nn.gelu(gate_part, approximate=True) * up_part).astype(jnp.bfloat16)
    partial_value = jnp.einsum("rk,ok->ro", gated, w_down_t, preferred_element_type=jnp.float32)
    (w_qkv_full,), summed = fetch_group(
        n_tok, 2, (w_qkv.reshape(w_qkv.shape[0], -1),), None,
        partial_value.reshape(requests, draft_slots, model_width).astype(jnp.bfloat16),
    )
    stream_three = summed.astype(jnp.float32) + stream_two
    normed_three = normed_rows(stream_three, gain_next)
    projected = jnp.dot(
        normed_three,
        w_qkv_full.reshape(w_qkv_full.shape[0], -1),
        preferred_element_type=jnp.float32,
    )
    projected = projected.astype(jnp.bfloat16).reshape(requests, draft_slots, 3, head_width)
    next_qkv = jnp.transpose(projected, (2, 0, 1, 3))
    out_hidden = lax.dynamic_slice_in_dim(stream_three, offset, share_rows, 1).astype(jnp.bfloat16)
    return (out_hidden, next_qkv)


def solution(mesh):
    in_specs = (
        P("tok", "grp", None),
        P(None, "tok", None, "grp"),
        P("tok", None, None, "grp"),
        P("tok", None, None, "grp"),
        P("tok", None),
        P("tok"),
        P("tok"),
        P("tok"),
        P("tok", None, None),
        P(None, "grp"),
        P(),
        P(),
        P(),
        P("grp", "tok"),
        P("tok", "grp"),
        P("grp", "tok"),
        P("tok", "grp"),
        P("tok", "grp"),
        P("grp", "tok"),
        P("tok", None, "grp"),
    )
    out_specs = (P("tok", "grp", None), P(None, "tok", None, "grp"))
    return jax.shard_map(shards, mesh=mesh, in_specs=in_specs, out_specs=out_specs, check_vma=False)
```

```python
import functools

import jax
import jax.numpy as jnp
from jax import lax
from jax.experimental import pallas as pl
from jax.experimental.pallas import tpu as pltpu
from jax.sharding import PartitionSpec as P

DH = 64


def ancestor_table(parent_ids):
    count_slots = parent_ids.shape[0]
    slot_ids = jnp.arange(count_slots, dtype=jnp.int32)
    ancestors = jnp.eye(count_slots, dtype=jnp.float32) + (
        parent_ids[:, None] == slot_ids[None, :]
    ).astype(jnp.float32)
    for repeat in range(max(1, count_slots.bit_length())):
        ancestors = jnp.minimum(jnp.dot(ancestors, ancestors, precision=lax.Precision.HIGHEST), 1.0)
    return ancestors


def rms_scale(stream, gain_vec):
    mean_square = jnp.mean(stream * stream, axis=-1, keepdims=True)
    return (stream * lax.rsqrt(mean_square + 1e-06) * gain_vec).astype(jnp.bfloat16)


def draft_attention(projected, cached, parent_ids, draft_count, length, bucket_ids, bias_table):
    requests, draft_slots, head_width = (projected.shape[1], projected.shape[2], projected.shape[3])
    local_heads = bias_table.shape[1]
    head_size = head_width // local_heads
    queries = projected[0].reshape(requests, draft_slots, local_heads, head_size)
    draft_keys = projected[1].reshape(requests, draft_slots, local_heads, head_size)
    draft_values = projected[2].reshape(requests, draft_slots, local_heads, head_size)
    cache_keys = cached[:, 0].reshape(requests, -1, local_heads, head_size)
    cache_values = cached[:, 1].reshape(requests, -1, local_heads, head_size)
    cache_scores = jnp.einsum(
        "rihd,rphd->rhip", queries, cache_keys, preferred_element_type=jnp.float32
    )
    cache_scores = cache_scores + bias_table[-1][None, :, None, None]
    cache_live = jnp.arange(cache_keys.shape[1], dtype=jnp.int32)[None, :] < length[:, None]
    cache_scores = jnp.where(cache_live[:, None, None, :], cache_scores, -1e30)
    onehot = (bucket_ids[..., None] == jnp.arange(bias_table.shape[0], dtype=jnp.int32)).astype(
        jnp.float32
    )
    draft_bias = jnp.einsum("rijb,bh->rhij", onehot, bias_table, precision=lax.Precision.HIGHEST)
    draft_scores = (
        jnp.einsum("rihd,rjhd->rhij", queries, draft_keys, preferred_element_type=jnp.float32)
        + draft_bias
    )
    ancestors = jax.vmap(ancestor_table)(parent_ids)
    draft_live = (ancestors > 0.5) & (
        jnp.arange(draft_slots, dtype=jnp.int32)[None, None, :] < draft_count[:, None, None]
    )
    draft_scores = jnp.where(draft_live[:, None], draft_scores, -1e30)
    highest = jnp.maximum(cache_scores.max(-1, keepdims=True), draft_scores.max(-1, keepdims=True))
    exp_cache = jnp.exp(cache_scores - highest)
    exp_draft = jnp.exp(draft_scores - highest)
    denominator = exp_cache.sum(-1, keepdims=True) + exp_draft.sum(-1, keepdims=True)
    weights_cache = (exp_cache / denominator).astype(jnp.bfloat16)
    weights_draft = (exp_draft / denominator).astype(jnp.bfloat16)
    attended = jnp.einsum(
        "rhip,rphd->rihd", weights_cache, cache_values, preferred_element_type=jnp.float32
    )
    attended = attended + jnp.einsum(
        "rhij,rjhd->rihd", weights_draft, draft_values, preferred_element_type=jnp.float32
    )
    return attended.astype(jnp.bfloat16).reshape(requests * draft_slots, head_width)


def cross_attention(query_rows, cached, length):
    requests, draft_slots, head_width = query_rows.shape
    local_heads = head_width // DH
    queries = query_rows.reshape(requests, draft_slots, local_heads, DH)
    enc_keys = cached[:, 0].reshape(requests, -1, local_heads, DH)
    enc_values = cached[:, 1].reshape(requests, -1, local_heads, DH)
    scores = jnp.einsum("rihd,rphd->rhip", queries, enc_keys, preferred_element_type=jnp.float32)
    live = jnp.arange(enc_keys.shape[1], dtype=jnp.int32)[None, :] < length[:, None]
    scores = jnp.where(live[:, None, None, :], scores, -1e30)
    highest = scores.max(-1, keepdims=True)
    exp_scores = jnp.exp(scores - highest)
    weights = (exp_scores / exp_scores.sum(-1, keepdims=True)).astype(jnp.bfloat16)
    attended = jnp.einsum(
        "rhip,rphd->rihd", weights, enc_values, preferred_element_type=jnp.float32
    )
    return attended.astype(jnp.bfloat16).reshape(requests * draft_slots, head_width)


def gather_kernel(n_chips, n_in, n_grp, *refs):
    srcs = refs[:n_in]
    if n_grp:
        summand = refs[n_in]
        outs = refs[n_in + 1:2 * n_in + 1]
        summed = refs[2 * n_in + 1]
        rest = refs[2 * n_in + 2:]
        send_sems, recv_sems, local_sems, fwd_send, fwd_recv, parts_in, rs_send, rs_recv, ag_send, ag_recv = rest
    else:
        outs = refs[n_in:2 * n_in]
        send_sems, recv_sems, local_sems, fwd_send, fwd_recv = refs[2 * n_in:]
    grp = lax.axis_index("grp")
    me = lax.axis_index("tok")
    chip = me // 2
    core = me % 2
    sibling = chip * 2 + (1 - core)
    mesh_id = pl.DeviceIdType.MESH

    barrier = pltpu.get_barrier_semaphore()
    for k in range(1, n_chips):
        peer = lax.rem(chip + k, n_chips) * 2 + core
        pl.semaphore_signal(barrier, inc=1, device_id=(grp, peer), device_id_type=mesh_id)
    pl.semaphore_signal(barrier, inc=1, device_id=(grp, sibling), device_id_type=mesh_id)
    for j in range(1, max(n_grp, 1)):
        pl.semaphore_signal(
            barrier, inc=1, device_id=(lax.rem(grp + j, n_grp), me), device_id_type=mesh_id
        )
    pl.semaphore_wait(barrier, n_chips + max(n_grp - 1, 0))

    locals_ = [
        pltpu.make_async_copy(srcs[i], outs[i].at[chip, core], local_sems.at[i]) for i in range(n_in)
    ]
    for copy in locals_:
        copy.start()

    def remote(i, k):
        other = lax.rem(chip + k, n_chips)
        return pltpu.make_async_remote_copy(
            src_ref=srcs[i],
            dst_ref=outs[i].at[chip, core],
            send_sem=send_sems.at[i, k],
            recv_sem=recv_sems.at[i, chip],
            device_id=(grp, other * 2 + core),
            device_id_type=mesh_id,
        )

    def send(k, carry):
        for i in range(n_in):
            remote(i, k).start()
        return carry

    lax.fori_loop(1, n_chips, send, 0)

    if n_grp:
        quarter = summand.shape[1] // n_grp

        def scatter(j):
            target = lax.rem(grp + j, n_grp)
            return pltpu.make_async_remote_copy(
                src_ref=summand.at[:, pl.ds(target * quarter, quarter)],
                dst_ref=parts_in.at[grp],
                send_sem=rs_send.at[j],
                recv_sem=rs_recv.at[grp],
                device_id=(target, me),
                device_id_type=mesh_id,
            )

        for j in range(1, n_grp):
            scatter(j).start()
        for j in range(1, n_grp):
            scatter(j).wait_send()
            source = lax.rem(grp + j, n_grp)
            pltpu.make_async_copy(parts_in.at[source], parts_in.at[source], rs_recv.at[source]).wait()
        mine = pl.ds(grp * quarter, quarter)
        total = summand[:, mine, :].astype(jnp.float32)
        for j in range(1, n_grp):
            total = total + parts_in[lax.rem(grp + j, n_grp)].astype(jnp.float32)
        summed[:, mine, :] = total.astype(summed.dtype)

        def spread(j):
            target = lax.rem(grp + j, n_grp)
            return pltpu.make_async_remote_copy(
                src_ref=summed.at[:, mine],
                dst_ref=summed.at[:, mine],
                send_sem=ag_send.at[j],
                recv_sem=ag_recv.at[grp],
                device_id=(target, me),
                device_id_type=mesh_id,
            )

        for j in range(1, n_grp):
            spread(j).start()

    def forward(i, c):
        return pltpu.make_async_remote_copy(
            src_ref=outs[i].at[c, core],
            dst_ref=outs[i].at[c, core],
            send_sem=fwd_send.at[i, c],
            recv_sem=fwd_recv.at[i, c],
            device_id=(grp, sibling),
            device_id_type=mesh_id,
        )

    for i in range(n_in):
        locals_[i].wait()
        forward(i, chip).start()

    def arrive(k, carry):
        other = lax.rem(chip + k, n_chips)
        for i in range(n_in):
            pltpu.make_async_copy(
                srcs[i], outs[i].at[other, core], recv_sems.at[i, other]
            ).wait()
            forward(i, other).start()
        for i in range(n_in):
            remote(i, k).wait_send()
        return carry

    lax.fori_loop(1, n_chips, arrive, 0)

    def land(c, carry):
        for i in range(n_in):
            forward(i, c).wait_send()
            pltpu.make_async_copy(
                outs[i].at[c, core], outs[i].at[c, 1 - core], fwd_recv.at[i, c]
            ).wait()
        return carry

    lax.fori_loop(0, n_chips, land, 0)

    if n_grp:
        for j in range(1, n_grp):
            spread(j).wait_send()
            source = lax.rem(grp + j, n_grp)
            rows = pl.ds(source * quarter, quarter)
            pltpu.make_async_copy(summed.at[:, rows], summed.at[:, rows], ag_recv.at[source]).wait()


def fetch_group(n_tok, collective_id, parts, after, summand=None):
    if summand is None:
        parts = list(lax.optimization_barrier((tuple(parts), after))[0])
    n_chips = n_tok // 2
    n_in = len(parts)
    n_grp = 0 if summand is None else lax.axis_size("grp")
    moved = 2 * n_tok * sum(p.size for p in parts) * parts[0].dtype.itemsize
    out_shape = [jax.ShapeDtypeStruct((n_chips, 2) + p.shape, p.dtype) for p in parts]
    out_specs = [pl.BlockSpec(memory_space=pl.ANY) for _ in parts]
    in_specs = [pl.BlockSpec(memory_space=pl.ANY)] * n_in
    operands = list(parts)
    scratch = [
        pltpu.SemaphoreType.DMA((n_in, n_chips)),
        pltpu.SemaphoreType.DMA((n_in, n_chips)),
        pltpu.SemaphoreType.DMA((n_in,)),
        pltpu.SemaphoreType.DMA((n_in, n_chips)),
        pltpu.SemaphoreType.DMA((n_in, n_chips)),
    ]
    if n_grp:
        requests, slots, width = summand.shape
        operands.append(summand)
        in_specs.append(pl.BlockSpec(memory_space=pltpu.VMEM))
        out_shape.append(jax.ShapeDtypeStruct(summand.shape, summand.dtype))
        out_specs.append(pl.BlockSpec(memory_space=pltpu.VMEM))
        scratch += [
            pltpu.VMEM((n_grp, requests, slots // n_grp, width), summand.dtype),
            pltpu.SemaphoreType.DMA((n_grp,)),
            pltpu.SemaphoreType.DMA((n_grp,)),
            pltpu.SemaphoreType.DMA((n_grp,)),
            pltpu.SemaphoreType.DMA((n_grp,)),
        ]
    results = pl.pallas_call(
        functools.partial(gather_kernel, n_chips, n_in, n_grp),
        out_shape=tuple(out_shape),
        in_specs=in_specs,
        out_specs=tuple(out_specs),
        scratch_shapes=scratch,
        compiler_params=pltpu.CompilerParams(collective_id=collective_id, has_side_effects=True),
        cost_estimate=pl.CostEstimate(flops=0, transcendentals=0, bytes_accessed=moved),
    )(*operands)
    gathered = [g.reshape((n_tok * g.shape[2],) + g.shape[3:]) for g in results[:n_in]]
    if n_grp:
        return gathered, results[n_in]
    return gathered

def doubling_gather(block, n_tok):
    position = lax.axis_index("tok")
    held = block[None]
    step = 1
    while step < n_tok:
        arrived = lax.ppermute(held, "tok", perm=[(i, i ^ step) for i in range(n_tok)])
        upper = (position // step) % 2 == 1
        held = jnp.where(
            upper,
            jnp.concatenate([arrived, held], axis=0),
            jnp.concatenate([held, arrived], axis=0),
        )
        step *= 2
    return held.reshape((n_tok * block.shape[0],) + block.shape[1:])


def layer_sum(summand, base_full):
    return lax.psum(summand.astype(jnp.bfloat16), "grp").astype(jnp.float32) + base_full


def normed_rows(stream, gain_vec):
    scaled = rms_scale(stream, gain_vec)
    return scaled.reshape(-1, scaled.shape[-1])


def shards(
    hidden,
    draft_qkv,
    self_cache,
    cross_cache,
    parents,
    counts,
    self_len,
    enc_len,
    buckets,
    bias_table,
    gain_cross,
    gain_ffn,
    gain_next,
    w_out_self,
    w_query_cross,
    w_out_cross,
    w_gate,
    w_up,
    w_down,
    w_qkv,
):
    requests, share_rows, model_width = hidden.shape
    draft_slots = draft_qkv.shape[2]
    head_width = draft_qkv.shape[3]
    self_context = draft_attention(
        draft_qkv, self_cache, parents, counts, self_len, buckets, bias_table
    )
    w_out_self_t = doubling_gather(w_out_self.T, lax.axis_size("tok"))
    partial_value = jnp.einsum(
        "rk,ok->ro", self_context, w_out_self_t, preferred_element_type=jnp.float32
    )
    partial_value = partial_value.reshape(requests, draft_slots, model_width)
    own_rows = hidden.astype(jnp.float32)
    offset = lax.axis_index("grp") * share_rows
    placed = lax.dynamic_update_slice(
        jnp.zeros((requests, draft_slots, model_width), jnp.float32), own_rows, (0, offset, 0)
    )
    summand = partial_value + placed
    n_tok = lax.axis_size("tok")
    (w_query_full, w_out_cross_t, w_gate_full), summed = fetch_group(
        n_tok, 0, (w_query_cross, w_out_cross.T, w_gate), None, summand.astype(jnp.bfloat16)
    )
    stream_one = summed.astype(jnp.float32)
    normed_one = normed_rows(stream_one, gain_cross)
    cross_query = jnp.dot(normed_one, w_query_full, preferred_element_type=jnp.float32)
    cross_query = cross_query.astype(jnp.bfloat16).reshape(requests, draft_slots, head_width)
    cross_context = cross_attention(cross_query, cross_cache, enc_len)
    partial_value = jnp.einsum(
        "rk,ok->ro", cross_context, w_out_cross_t, preferred_element_type=jnp.float32
    )
    (w_up_full, w_down_t), summed = fetch_group(
        n_tok, 1, (w_up, w_down.T), None,
        partial_value.reshape(requests, draft_slots, model_width).astype(jnp.bfloat16),
    )
    stream_two = summed.astype(jnp.float32) + stream_one
    normed_two = normed_rows(stream_two, gain_ffn)
    gate_part = jnp.dot(normed_two, w_gate_full, preferred_element_type=jnp.float32)
    up_part = jnp.dot(normed_two, w_up_full, preferred_element_type=jnp.float32)
    gated = (jax.nn.gelu(gate_part, approximate=True) * up_part).astype(jnp.bfloat16)
    partial_value = jnp.einsum("rk,ok->ro", gated, w_down_t, preferred_element_type=jnp.float32)
    (w_qkv_full,), summed = fetch_group(
        n_tok, 2, (w_qkv.reshape(w_qkv.shape[0], -1),), None,
        partial_value.reshape(requests, draft_slots, model_width).astype(jnp.bfloat16),
    )
    stream_three = summed.astype(jnp.float32) + stream_two
    normed_three = normed_rows(stream_three, gain_next)
    projected = jnp.dot(
        normed_three,
        w_qkv_full.reshape(w_qkv_full.shape[0], -1),
        preferred_element_type=jnp.float32,
    )
    projected = projected.astype(jnp.bfloat16).reshape(requests, draft_slots, 3, head_width)
    next_qkv = jnp.transpose(projected, (2, 0, 1, 3))
    out_hidden = lax.dynamic_slice_in_dim(stream_three, offset, share_rows, 1).astype(jnp.bfloat16)
    return (out_hidden, next_qkv)


def solution(mesh):
    in_specs = (
        P("tok", "grp", None),
        P(None, "tok", None, "grp"),
        P("tok", None, None, "grp"),
        P("tok", None, None, "grp"),
        P("tok", None),
        P("tok"),
        P("tok"),
        P("tok"),
        P("tok", None, None),
        P(None, "grp"),
        P(),
        P(),
        P(),
        P("grp", "tok"),
        P("tok", "grp"),
        P("grp", "tok"),
        P("tok", "grp"),
        P("tok", "grp"),
        P("grp", "tok"),
        P("tok", None, "grp"),
    )
    out_specs = (P("tok", "grp", None), P(None, "tok", None, "grp"))
    return jax.shard_map(shards, mesh=mesh, in_specs=in_specs, out_specs=out_specs, check_vma=False)
```

```python
import functools

import jax
import jax.numpy as jnp
from jax import lax
from jax.experimental import pallas as pl
from jax.experimental.pallas import tpu as pltpu
from jax.sharding import PartitionSpec as P

DH = 64


def ancestor_table(parent_ids):
    count_slots = parent_ids.shape[0]
    slot_ids = jnp.arange(count_slots, dtype=jnp.int32)
    ancestors = jnp.eye(count_slots, dtype=jnp.float32) + (
        parent_ids[:, None] == slot_ids[None, :]
    ).astype(jnp.float32)
    for repeat in range(max(1, count_slots.bit_length())):
        ancestors = jnp.minimum(jnp.dot(ancestors, ancestors, precision=lax.Precision.HIGHEST), 1.0)
    return ancestors


def rms_scale(stream, gain_vec):
    mean_square = jnp.mean(stream * stream, axis=-1, keepdims=True)
    return (stream * lax.rsqrt(mean_square + 1e-06) * gain_vec).astype(jnp.bfloat16)


def draft_attention(projected, cached, parent_ids, draft_count, length, bucket_ids, bias_table):
    requests, draft_slots, head_width = (projected.shape[1], projected.shape[2], projected.shape[3])
    local_heads = bias_table.shape[1]
    head_size = head_width // local_heads
    queries = projected[0].reshape(requests, draft_slots, local_heads, head_size)
    draft_keys = projected[1].reshape(requests, draft_slots, local_heads, head_size)
    draft_values = projected[2].reshape(requests, draft_slots, local_heads, head_size)
    cache_keys = cached[:, 0].reshape(requests, -1, local_heads, head_size)
    cache_values = cached[:, 1].reshape(requests, -1, local_heads, head_size)
    cache_scores = jnp.einsum(
        "rihd,rphd->rhip", queries, cache_keys, preferred_element_type=jnp.float32
    )
    cache_scores = cache_scores + bias_table[-1][None, :, None, None]
    cache_live = jnp.arange(cache_keys.shape[1], dtype=jnp.int32)[None, :] < length[:, None]
    cache_scores = jnp.where(cache_live[:, None, None, :], cache_scores, -1e30)
    onehot = (bucket_ids[..., None] == jnp.arange(bias_table.shape[0], dtype=jnp.int32)).astype(
        jnp.float32
    )
    draft_bias = jnp.einsum("rijb,bh->rhij", onehot, bias_table, precision=lax.Precision.HIGHEST)
    draft_scores = (
        jnp.einsum("rihd,rjhd->rhij", queries, draft_keys, preferred_element_type=jnp.float32)
        + draft_bias
    )
    ancestors = jax.vmap(ancestor_table)(parent_ids)
    draft_live = (ancestors > 0.5) & (
        jnp.arange(draft_slots, dtype=jnp.int32)[None, None, :] < draft_count[:, None, None]
    )
    draft_scores = jnp.where(draft_live[:, None], draft_scores, -1e30)
    highest = jnp.maximum(cache_scores.max(-1, keepdims=True), draft_scores.max(-1, keepdims=True))
    exp_cache = jnp.exp(cache_scores - highest)
    exp_draft = jnp.exp(draft_scores - highest)
    denominator = exp_cache.sum(-1, keepdims=True) + exp_draft.sum(-1, keepdims=True)
    weights_cache = (exp_cache / denominator).astype(jnp.bfloat16)
    weights_draft = (exp_draft / denominator).astype(jnp.bfloat16)
    attended = jnp.einsum(
        "rhip,rphd->rihd", weights_cache, cache_values, preferred_element_type=jnp.float32
    )
    attended = attended + jnp.einsum(
        "rhij,rjhd->rihd", weights_draft, draft_values, preferred_element_type=jnp.float32
    )
    return attended.astype(jnp.bfloat16).reshape(requests * draft_slots, head_width)


def cross_attention(query_rows, cached, length):
    requests, draft_slots, head_width = query_rows.shape
    local_heads = head_width // DH
    queries = query_rows.reshape(requests, draft_slots, local_heads, DH)
    enc_keys = cached[:, 0].reshape(requests, -1, local_heads, DH)
    enc_values = cached[:, 1].reshape(requests, -1, local_heads, DH)
    scores = jnp.einsum("rihd,rphd->rhip", queries, enc_keys, preferred_element_type=jnp.float32)
    live = jnp.arange(enc_keys.shape[1], dtype=jnp.int32)[None, :] < length[:, None]
    scores = jnp.where(live[:, None, None, :], scores, -1e30)
    highest = scores.max(-1, keepdims=True)
    exp_scores = jnp.exp(scores - highest)
    weights = (exp_scores / exp_scores.sum(-1, keepdims=True)).astype(jnp.bfloat16)
    attended = jnp.einsum(
        "rhip,rphd->rihd", weights, enc_values, preferred_element_type=jnp.float32
    )
    return attended.astype(jnp.bfloat16).reshape(requests * draft_slots, head_width)


def gather_kernel(n_chips, n_in, n_grp, *refs):
    srcs = refs[:n_in]
    if n_grp:
        summand = refs[n_in]
        outs = refs[n_in + 1:2 * n_in + 1]
        summed = refs[2 * n_in + 1]
        rest = refs[2 * n_in + 2:]
        send_sems, recv_sems, local_sems, fwd_send, fwd_recv, parts_in, rs_send, rs_recv, ag_send, ag_recv = rest
    else:
        outs = refs[n_in:2 * n_in]
        send_sems, recv_sems, local_sems, fwd_send, fwd_recv = refs[2 * n_in:]
    grp = lax.axis_index("grp")
    me = lax.axis_index("tok")
    chip = me // 2
    core = me % 2
    sibling = chip * 2 + (1 - core)
    mesh_id = pl.DeviceIdType.MESH

    barrier = pltpu.get_barrier_semaphore()
    for k in range(1, n_chips):
        peer = lax.rem(chip + k, n_chips) * 2 + core
        pl.semaphore_signal(barrier, inc=1, device_id=(grp, peer), device_id_type=mesh_id)
    pl.semaphore_signal(barrier, inc=1, device_id=(grp, sibling), device_id_type=mesh_id)
    for j in range(1, max(n_grp, 1)):
        pl.semaphore_signal(
            barrier, inc=1, device_id=(lax.rem(grp + j, n_grp), me), device_id_type=mesh_id
        )
    pl.semaphore_wait(barrier, n_chips + max(n_grp - 1, 0))

    locals_ = [
        pltpu.make_async_copy(srcs[i], outs[i].at[chip, core], local_sems.at[i]) for i in range(n_in)
    ]
    for copy in locals_:
        copy.start()

    def remote(i, k):
        other = lax.rem(chip + k, n_chips)
        return pltpu.make_async_remote_copy(
            src_ref=srcs[i],
            dst_ref=outs[i].at[chip, core],
            send_sem=send_sems.at[i, k],
            recv_sem=recv_sems.at[i, chip],
            device_id=(grp, other * 2 + core),
            device_id_type=mesh_id,
        )

    def send(k, carry):
        for i in range(n_in):
            remote(i, k).start()
        return carry

    lax.fori_loop(1, n_chips, send, 0)

    if n_grp:
        quarter = summand.shape[1] // n_grp

        def scatter(j):
            target = lax.rem(grp + j, n_grp)
            return pltpu.make_async_remote_copy(
                src_ref=summand.at[:, pl.ds(target * quarter, quarter)],
                dst_ref=parts_in.at[grp],
                send_sem=rs_send.at[j],
                recv_sem=rs_recv.at[grp],
                device_id=(target, me),
                device_id_type=mesh_id,
            )

        for j in range(1, n_grp):
            scatter(j).start()
        for j in range(1, n_grp):
            scatter(j).wait_send()
            source = lax.rem(grp + j, n_grp)
            pltpu.make_async_copy(parts_in.at[source], parts_in.at[source], rs_recv.at[source]).wait()
        mine = pl.ds(grp * quarter, quarter)
        total = summand[:, mine, :].astype(jnp.float32)
        for j in range(1, n_grp):
            total = total + parts_in[lax.rem(grp + j, n_grp)].astype(jnp.float32)
        summed[:, mine, :] = total.astype(summed.dtype)

        def spread(j):
            target = lax.rem(grp + j, n_grp)
            return pltpu.make_async_remote_copy(
                src_ref=summed.at[:, mine],
                dst_ref=summed.at[:, mine],
                send_sem=ag_send.at[j],
                recv_sem=ag_recv.at[grp],
                device_id=(target, me),
                device_id_type=mesh_id,
            )

        for j in range(1, n_grp):
            spread(j).start()

    def forward(i, c):
        return pltpu.make_async_remote_copy(
            src_ref=outs[i].at[c, core],
            dst_ref=outs[i].at[c, core],
            send_sem=fwd_send.at[i, c],
            recv_sem=fwd_recv.at[i, c],
            device_id=(grp, sibling),
            device_id_type=mesh_id,
        )

    for i in range(n_in):
        locals_[i].wait()
        forward(i, chip).start()

    def arrive(k, carry):
        other = lax.rem(chip + k, n_chips)
        for i in range(n_in):
            pltpu.make_async_copy(
                srcs[i], outs[i].at[other, core], recv_sems.at[i, other]
            ).wait()
            forward(i, other).start()
        for i in range(n_in):
            remote(i, k).wait_send()
        return carry

    lax.fori_loop(1, n_chips, arrive, 0)

    def land(c, carry):
        for i in range(n_in):
            forward(i, c).wait_send()
            pltpu.make_async_copy(
                outs[i].at[c, core], outs[i].at[c, 1 - core], fwd_recv.at[i, c]
            ).wait()
        return carry

    lax.fori_loop(0, n_chips, land, 0)

    if n_grp:
        for j in range(1, n_grp):
            spread(j).wait_send()
            source = lax.rem(grp + j, n_grp)
            rows = pl.ds(source * quarter, quarter)
            pltpu.make_async_copy(summed.at[:, rows], summed.at[:, rows], ag_recv.at[source]).wait()


def fetch_group(n_tok, collective_id, parts, after, summand=None):
    if summand is None:
        parts = list(lax.optimization_barrier((tuple(parts), after))[0])
    n_chips = n_tok // 2
    n_in = len(parts)
    n_grp = 0 if summand is None else lax.axis_size("grp")
    moved = 2 * n_tok * sum(p.size for p in parts) * parts[0].dtype.itemsize
    out_shape = [jax.ShapeDtypeStruct((n_chips, 2) + p.shape, p.dtype) for p in parts]
    out_specs = [pl.BlockSpec(memory_space=pl.ANY) for _ in parts]
    in_specs = [pl.BlockSpec(memory_space=pl.ANY)] * n_in
    operands = list(parts)
    scratch = [
        pltpu.SemaphoreType.DMA((n_in, n_chips)),
        pltpu.SemaphoreType.DMA((n_in, n_chips)),
        pltpu.SemaphoreType.DMA((n_in,)),
        pltpu.SemaphoreType.DMA((n_in, n_chips)),
        pltpu.SemaphoreType.DMA((n_in, n_chips)),
    ]
    if n_grp:
        requests, slots, width = summand.shape
        operands.append(summand)
        in_specs.append(pl.BlockSpec(memory_space=pltpu.VMEM))
        out_shape.append(jax.ShapeDtypeStruct(summand.shape, summand.dtype))
        out_specs.append(pl.BlockSpec(memory_space=pltpu.VMEM))
        scratch += [
            pltpu.VMEM((n_grp, requests, slots // n_grp, width), summand.dtype),
            pltpu.SemaphoreType.DMA((n_grp,)),
            pltpu.SemaphoreType.DMA((n_grp,)),
            pltpu.SemaphoreType.DMA((n_grp,)),
            pltpu.SemaphoreType.DMA((n_grp,)),
        ]
    results = pl.pallas_call(
        functools.partial(gather_kernel, n_chips, n_in, n_grp),
        out_shape=tuple(out_shape),
        in_specs=in_specs,
        out_specs=tuple(out_specs),
        scratch_shapes=scratch,
        compiler_params=pltpu.CompilerParams(collective_id=collective_id, has_side_effects=True),
        cost_estimate=pl.CostEstimate(flops=0, transcendentals=0, bytes_accessed=moved),
    )(*operands)
    gathered = [g.reshape((n_tok * g.shape[2],) + g.shape[3:]) for g in results[:n_in]]
    if n_grp:
        return gathered, results[n_in]
    return gathered

def direct_kernel(n_tok, src_ref, out_ref, send_sems, recv_sems, local_sem):
    grp = lax.axis_index("grp")
    me = lax.axis_index("tok")
    mesh_id = pl.DeviceIdType.MESH
    barrier = pltpu.get_barrier_semaphore()
    for k in range(1, n_tok):
        pl.semaphore_signal(
            barrier, inc=1, device_id=(grp, lax.rem(me + k, n_tok)), device_id_type=mesh_id
        )
    pl.semaphore_wait(barrier, n_tok - 1)
    local = pltpu.make_async_copy(src_ref, out_ref.at[me], local_sem)
    local.start()

    def remote(k):
        return pltpu.make_async_remote_copy(
            src_ref=src_ref,
            dst_ref=out_ref.at[me],
            send_sem=send_sems.at[k],
            recv_sem=recv_sems.at[me],
            device_id=(grp, lax.rem(me + k, n_tok)),
            device_id_type=mesh_id,
        )

    def send(k, carry):
        remote(k).start()
        return carry

    lax.fori_loop(1, n_tok, send, 0)

    def arrive(k, carry):
        other = lax.rem(me + k, n_tok)
        pltpu.make_async_copy(src_ref, out_ref.at[other], recv_sems.at[other]).wait()
        remote(k).wait_send()
        return carry

    lax.fori_loop(1, n_tok, arrive, 0)
    local.wait()


def direct_gather(block, n_tok, after):
    block, _ = lax.optimization_barrier((block, after))
    gathered = pl.pallas_call(
        functools.partial(direct_kernel, n_tok),
        out_shape=jax.ShapeDtypeStruct((n_tok,) + block.shape, block.dtype),
        in_specs=[pl.BlockSpec(memory_space=pl.ANY)],
        out_specs=pl.BlockSpec(memory_space=pl.ANY),
        scratch_shapes=[
            pltpu.SemaphoreType.DMA((n_tok,)),
            pltpu.SemaphoreType.DMA((n_tok,)),
            pltpu.SemaphoreType.DMA(()),
        ],
        compiler_params=pltpu.CompilerParams(collective_id=3, has_side_effects=True),
        cost_estimate=pl.CostEstimate(
            flops=0, transcendentals=0, bytes_accessed=2 * n_tok * block.size * block.dtype.itemsize
        ),
    )(block)
    return gathered.reshape((n_tok * block.shape[0],) + block.shape[1:])


def layer_sum(summand, base_full):
    return lax.psum(summand.astype(jnp.bfloat16), "grp").astype(jnp.float32) + base_full


def normed_rows(stream, gain_vec):
    scaled = rms_scale(stream, gain_vec)
    return scaled.reshape(-1, scaled.shape[-1])


def shards(
    hidden,
    draft_qkv,
    self_cache,
    cross_cache,
    parents,
    counts,
    self_len,
    enc_len,
    buckets,
    bias_table,
    gain_cross,
    gain_ffn,
    gain_next,
    w_out_self,
    w_query_cross,
    w_out_cross,
    w_gate,
    w_up,
    w_down,
    w_qkv,
):
    requests, share_rows, model_width = hidden.shape
    draft_slots = draft_qkv.shape[2]
    head_width = draft_qkv.shape[3]
    self_context = draft_attention(
        draft_qkv, self_cache, parents, counts, self_len, buckets, bias_table
    )
    w_out_self_t = direct_gather(w_out_self.T, lax.axis_size("tok"), self_context)
    partial_value = jnp.einsum(
        "rk,ok->ro", self_context, w_out_self_t, preferred_element_type=jnp.float32
    )
    partial_value = partial_value.reshape(requests, draft_slots, model_width)
    own_rows = hidden.astype(jnp.float32)
    offset = lax.axis_index("grp") * share_rows
    placed = lax.dynamic_update_slice(
        jnp.zeros((requests, draft_slots, model_width), jnp.float32), own_rows, (0, offset, 0)
    )
    summand = partial_value + placed
    n_tok = lax.axis_size("tok")
    (w_query_full, w_out_cross_t, w_gate_full), summed = fetch_group(
        n_tok, 0, (w_query_cross, w_out_cross.T, w_gate), None, summand.astype(jnp.bfloat16)
    )
    stream_one = summed.astype(jnp.float32)
    normed_one = normed_rows(stream_one, gain_cross)
    cross_query = jnp.dot(normed_one, w_query_full, preferred_element_type=jnp.float32)
    cross_query = cross_query.astype(jnp.bfloat16).reshape(requests, draft_slots, head_width)
    cross_context = cross_attention(cross_query, cross_cache, enc_len)
    partial_value = jnp.einsum(
        "rk,ok->ro", cross_context, w_out_cross_t, preferred_element_type=jnp.float32
    )
    (w_up_full, w_down_t), summed = fetch_group(
        n_tok, 1, (w_up, w_down.T), None,
        partial_value.reshape(requests, draft_slots, model_width).astype(jnp.bfloat16),
    )
    stream_two = summed.astype(jnp.float32) + stream_one
    normed_two = normed_rows(stream_two, gain_ffn)
    gate_part = jnp.dot(normed_two, w_gate_full, preferred_element_type=jnp.float32)
    up_part = jnp.dot(normed_two, w_up_full, preferred_element_type=jnp.float32)
    gated = (jax.nn.gelu(gate_part, approximate=True) * up_part).astype(jnp.bfloat16)
    partial_value = jnp.einsum("rk,ok->ro", gated, w_down_t, preferred_element_type=jnp.float32)
    (w_qkv_full,), summed = fetch_group(
        n_tok, 2, (w_qkv.reshape(w_qkv.shape[0], -1),), None,
        partial_value.reshape(requests, draft_slots, model_width).astype(jnp.bfloat16),
    )
    stream_three = summed.astype(jnp.float32) + stream_two
    normed_three = normed_rows(stream_three, gain_next)
    projected = jnp.dot(
        normed_three,
        w_qkv_full.reshape(w_qkv_full.shape[0], -1),
        preferred_element_type=jnp.float32,
    )
    projected = projected.astype(jnp.bfloat16).reshape(requests, draft_slots, 3, head_width)
    next_qkv = jnp.transpose(projected, (2, 0, 1, 3))
    out_hidden = lax.dynamic_slice_in_dim(stream_three, offset, share_rows, 1).astype(jnp.bfloat16)
    return (out_hidden, next_qkv)


def solution(mesh):
    in_specs = (
        P("tok", "grp", None),
        P(None, "tok", None, "grp"),
        P("tok", None, None, "grp"),
        P("tok", None, None, "grp"),
        P("tok", None),
        P("tok"),
        P("tok"),
        P("tok"),
        P("tok", None, None),
        P(None, "grp"),
        P(),
        P(),
        P(),
        P("grp", "tok"),
        P("tok", "grp"),
        P("grp", "tok"),
        P("tok", "grp"),
        P("tok", "grp"),
        P("grp", "tok"),
        P("tok", None, "grp"),
    )
    out_specs = (P("tok", "grp", None), P(None, "tok", None, "grp"))
    return jax.shard_map(shards, mesh=mesh, in_specs=in_specs, out_specs=out_specs, check_vma=False)
```

```python
import functools

import jax
import jax.numpy as jnp
from jax import lax
from jax.experimental import pallas as pl
from jax.experimental.pallas import tpu as pltpu
from jax.sharding import PartitionSpec as P

DH = 64


def ancestor_table(parent_ids):
    count_slots = parent_ids.shape[0]
    slot_ids = jnp.arange(count_slots, dtype=jnp.int32)
    ancestors = jnp.eye(count_slots, dtype=jnp.float32) + (
        parent_ids[:, None] == slot_ids[None, :]
    ).astype(jnp.float32)
    for repeat in range(max(1, count_slots.bit_length())):
        ancestors = jnp.minimum(jnp.dot(ancestors, ancestors, precision=lax.Precision.HIGHEST), 1.0)
    return ancestors


def rms_scale(stream, gain_vec):
    mean_square = jnp.mean(stream * stream, axis=-1, keepdims=True)
    return (stream * lax.rsqrt(mean_square + 1e-06) * gain_vec).astype(jnp.bfloat16)


def draft_attention(projected, cached, parent_ids, draft_count, length, bucket_ids, bias_table):
    requests, draft_slots, head_width = (projected.shape[1], projected.shape[2], projected.shape[3])
    local_heads = bias_table.shape[1]
    head_size = head_width // local_heads
    queries = projected[0].reshape(requests, draft_slots, local_heads, head_size)
    draft_keys = projected[1].reshape(requests, draft_slots, local_heads, head_size)
    draft_values = projected[2].reshape(requests, draft_slots, local_heads, head_size)
    cache_keys = cached[:, 0].reshape(requests, -1, local_heads, head_size)
    cache_values = cached[:, 1].reshape(requests, -1, local_heads, head_size)
    cache_scores = jnp.einsum(
        "rihd,rphd->rhip", queries, cache_keys, preferred_element_type=jnp.float32
    )
    cache_scores = cache_scores + bias_table[-1][None, :, None, None]
    cache_live = jnp.arange(cache_keys.shape[1], dtype=jnp.int32)[None, :] < length[:, None]
    cache_scores = jnp.where(cache_live[:, None, None, :], cache_scores, -1e30)
    onehot = (bucket_ids[..., None] == jnp.arange(bias_table.shape[0], dtype=jnp.int32)).astype(
        jnp.float32
    )
    draft_bias = jnp.einsum("rijb,bh->rhij", onehot, bias_table, precision=lax.Precision.HIGHEST)
    draft_scores = (
        jnp.einsum("rihd,rjhd->rhij", queries, draft_keys, preferred_element_type=jnp.float32)
        + draft_bias
    )
    ancestors = jax.vmap(ancestor_table)(parent_ids)
    draft_live = (ancestors > 0.5) & (
        jnp.arange(draft_slots, dtype=jnp.int32)[None, None, :] < draft_count[:, None, None]
    )
    draft_scores = jnp.where(draft_live[:, None], draft_scores, -1e30)
    highest = jnp.maximum(cache_scores.max(-1, keepdims=True), draft_scores.max(-1, keepdims=True))
    exp_cache = jnp.exp(cache_scores - highest)
    exp_draft = jnp.exp(draft_scores - highest)
    denominator = exp_cache.sum(-1, keepdims=True) + exp_draft.sum(-1, keepdims=True)
    weights_cache = (exp_cache / denominator).astype(jnp.bfloat16)
    weights_draft = (exp_draft / denominator).astype(jnp.bfloat16)
    attended = jnp.einsum(
        "rhip,rphd->rihd", weights_cache, cache_values, preferred_element_type=jnp.float32
    )
    attended = attended + jnp.einsum(
        "rhij,rjhd->rihd", weights_draft, draft_values, preferred_element_type=jnp.float32
    )
    return attended.astype(jnp.bfloat16).reshape(requests * draft_slots, head_width)


def cross_attention(query_rows, cached, length):
    requests, draft_slots, head_width = query_rows.shape
    local_heads = head_width // DH
    queries = query_rows.reshape(requests, draft_slots, local_heads, DH)
    enc_keys = cached[:, 0].reshape(requests, -1, local_heads, DH)
    enc_values = cached[:, 1].reshape(requests, -1, local_heads, DH)
    scores = jnp.einsum("rihd,rphd->rhip", queries, enc_keys, preferred_element_type=jnp.float32)
    live = jnp.arange(enc_keys.shape[1], dtype=jnp.int32)[None, :] < length[:, None]
    scores = jnp.where(live[:, None, None, :], scores, -1e30)
    highest = scores.max(-1, keepdims=True)
    exp_scores = jnp.exp(scores - highest)
    weights = (exp_scores / exp_scores.sum(-1, keepdims=True)).astype(jnp.bfloat16)
    attended = jnp.einsum(
        "rhip,rphd->rihd", weights, enc_values, preferred_element_type=jnp.float32
    )
    return attended.astype(jnp.bfloat16).reshape(requests * draft_slots, head_width)


def cross_kernel(len_ref, q_ref, kv_ref, o_ref):
    length = len_ref[pl.program_id(0)]
    q = q_ref[0]
    keys = kv_ref[0, 0]
    values = kv_ref[0, 1]
    live = lax.broadcasted_iota(jnp.int32, (q.shape[0], keys.shape[0]), 1) < length
    for h in range(q.shape[1] // DH):
        cols = slice(h * DH, (h + 1) * DH)
        scores = lax.dot_general(
            q[:, cols], keys[:, cols], (((1,), (1,)), ((), ())), preferred_element_type=jnp.float32
        )
        scores = jnp.where(live, scores, -1e30)
        exp_scores = jnp.exp(scores - scores.max(-1, keepdims=True))
        total = exp_scores.sum(-1, keepdims=True)
        unscaled = jnp.dot(
            exp_scores.astype(jnp.bfloat16), values[:, cols], preferred_element_type=jnp.float32
        )
        o_ref[0, :, cols] = (unscaled / total).astype(o_ref.dtype)


def cross_attention_kernel(query_rows, cached, length):
    requests, draft_slots, head_width = query_rows.shape
    positions = cached.shape[2]
    attended = pl.pallas_call(
        cross_kernel,
        out_shape=jax.ShapeDtypeStruct(query_rows.shape, jnp.bfloat16),
        grid_spec=pltpu.PrefetchScalarGridSpec(
            num_scalar_prefetch=1,
            grid=(requests,),
            in_specs=[
                pl.BlockSpec((1, draft_slots, head_width), lambda r, lens: (r, 0, 0)),
                pl.BlockSpec((1, 2, positions, head_width), lambda r, lens: (r, 0, 0, 0)),
            ],
            out_specs=pl.BlockSpec((1, draft_slots, head_width), lambda r, lens: (r, 0, 0)),
        ),
        cost_estimate=pl.CostEstimate(
            flops=4 * requests * draft_slots * positions * head_width,
            transcendentals=requests * draft_slots * positions * (head_width // DH),
            bytes_accessed=2 * cached.size + 4 * query_rows.size,
        ),
    )(length, query_rows, cached)
    return attended.reshape(requests * draft_slots, head_width)


def gather_kernel(n_chips, n_in, n_grp, *refs):
    srcs = refs[:n_in]
    if n_grp:
        summand = refs[n_in]
        outs = refs[n_in + 1:2 * n_in + 1]
        summed = refs[2 * n_in + 1]
        rest = refs[2 * n_in + 2:]
        send_sems, recv_sems, local_sems, fwd_send, fwd_recv, parts_in, rs_send, rs_recv, ag_send, ag_recv = rest
    else:
        outs = refs[n_in:2 * n_in]
        send_sems, recv_sems, local_sems, fwd_send, fwd_recv = refs[2 * n_in:]
    grp = lax.axis_index("grp")
    me = lax.axis_index("tok")
    chip = me // 2
    core = me % 2
    sibling = chip * 2 + (1 - core)
    mesh_id = pl.DeviceIdType.MESH

    barrier = pltpu.get_barrier_semaphore()
    for k in range(1, n_chips):
        peer = lax.rem(chip + k, n_chips) * 2 + core
        pl.semaphore_signal(barrier, inc=1, device_id=(grp, peer), device_id_type=mesh_id)
    pl.semaphore_signal(barrier, inc=1, device_id=(grp, sibling), device_id_type=mesh_id)
    for j in range(1, max(n_grp, 1)):
        pl.semaphore_signal(
            barrier, inc=1, device_id=(lax.rem(grp + j, n_grp), me), device_id_type=mesh_id
        )
    pl.semaphore_wait(barrier, n_chips + max(n_grp - 1, 0))

    locals_ = [
        pltpu.make_async_copy(srcs[i], outs[i].at[chip, core], local_sems.at[i]) for i in range(n_in)
    ]
    for copy in locals_:
        copy.start()

    def remote(i, k):
        other = lax.rem(chip + k, n_chips)
        return pltpu.make_async_remote_copy(
            src_ref=srcs[i],
            dst_ref=outs[i].at[chip, core],
            send_sem=send_sems.at[i, k],
            recv_sem=recv_sems.at[i, chip],
            device_id=(grp, other * 2 + core),
            device_id_type=mesh_id,
        )

    def send(k, carry):
        for i in range(n_in):
            remote(i, k).start()
        return carry

    lax.fori_loop(1, n_chips, send, 0)

    if n_grp:
        quarter = summand.shape[1] // n_grp

        def scatter(j):
            target = lax.rem(grp + j, n_grp)
            return pltpu.make_async_remote_copy(
                src_ref=summand.at[:, pl.ds(target * quarter, quarter)],
                dst_ref=parts_in.at[grp],
                send_sem=rs_send.at[j],
                recv_sem=rs_recv.at[grp],
                device_id=(target, me),
                device_id_type=mesh_id,
            )

        for j in range(1, n_grp):
            scatter(j).start()
        for j in range(1, n_grp):
            scatter(j).wait_send()
            source = lax.rem(grp + j, n_grp)
            pltpu.make_async_copy(parts_in.at[source], parts_in.at[source], rs_recv.at[source]).wait()
        mine = pl.ds(grp * quarter, quarter)
        total = summand[:, mine, :].astype(jnp.float32)
        for j in range(1, n_grp):
            total = total + parts_in[lax.rem(grp + j, n_grp)].astype(jnp.float32)
        summed[:, mine, :] = total.astype(summed.dtype)

        def spread(j):
            target = lax.rem(grp + j, n_grp)
            return pltpu.make_async_remote_copy(
                src_ref=summed.at[:, mine],
                dst_ref=summed.at[:, mine],
                send_sem=ag_send.at[j],
                recv_sem=ag_recv.at[grp],
                device_id=(target, me),
                device_id_type=mesh_id,
            )

        for j in range(1, n_grp):
            spread(j).start()

    def forward(i, c):
        return pltpu.make_async_remote_copy(
            src_ref=outs[i].at[c, core],
            dst_ref=outs[i].at[c, core],
            send_sem=fwd_send.at[i, c],
            recv_sem=fwd_recv.at[i, c],
            device_id=(grp, sibling),
            device_id_type=mesh_id,
        )

    for i in range(n_in):
        locals_[i].wait()
        forward(i, chip).start()

    def arrive(k, carry):
        other = lax.rem(chip + k, n_chips)
        for i in range(n_in):
            pltpu.make_async_copy(
                srcs[i], outs[i].at[other, core], recv_sems.at[i, other]
            ).wait()
            forward(i, other).start()
        for i in range(n_in):
            remote(i, k).wait_send()
        return carry

    lax.fori_loop(1, n_chips, arrive, 0)

    def land(c, carry):
        for i in range(n_in):
            forward(i, c).wait_send()
            pltpu.make_async_copy(
                outs[i].at[c, core], outs[i].at[c, 1 - core], fwd_recv.at[i, c]
            ).wait()
        return carry

    lax.fori_loop(0, n_chips, land, 0)

    if n_grp:
        for j in range(1, n_grp):
            spread(j).wait_send()
            source = lax.rem(grp + j, n_grp)
            rows = pl.ds(source * quarter, quarter)
            pltpu.make_async_copy(summed.at[:, rows], summed.at[:, rows], ag_recv.at[source]).wait()


def fetch_group(n_tok, collective_id, parts, after, summand=None):
    if summand is None:
        parts = list(lax.optimization_barrier((tuple(parts), after))[0])
    n_chips = n_tok // 2
    n_in = len(parts)
    n_grp = 0 if summand is None else lax.axis_size("grp")
    moved = 2 * n_tok * sum(p.size for p in parts) * parts[0].dtype.itemsize
    out_shape = [jax.ShapeDtypeStruct((n_chips, 2) + p.shape, p.dtype) for p in parts]
    out_specs = [pl.BlockSpec(memory_space=pl.ANY) for _ in parts]
    in_specs = [pl.BlockSpec(memory_space=pl.ANY)] * n_in
    operands = list(parts)
    scratch = [
        pltpu.SemaphoreType.DMA((n_in, n_chips)),
        pltpu.SemaphoreType.DMA((n_in, n_chips)),
        pltpu.SemaphoreType.DMA((n_in,)),
        pltpu.SemaphoreType.DMA((n_in, n_chips)),
        pltpu.SemaphoreType.DMA((n_in, n_chips)),
    ]
    if n_grp:
        requests, slots, width = summand.shape
        operands.append(summand)
        in_specs.append(pl.BlockSpec(memory_space=pltpu.VMEM))
        out_shape.append(jax.ShapeDtypeStruct(summand.shape, summand.dtype))
        out_specs.append(pl.BlockSpec(memory_space=pltpu.VMEM))
        scratch += [
            pltpu.VMEM((n_grp, requests, slots // n_grp, width), summand.dtype),
            pltpu.SemaphoreType.DMA((n_grp,)),
            pltpu.SemaphoreType.DMA((n_grp,)),
            pltpu.SemaphoreType.DMA((n_grp,)),
            pltpu.SemaphoreType.DMA((n_grp,)),
        ]
    results = pl.pallas_call(
        functools.partial(gather_kernel, n_chips, n_in, n_grp),
        out_shape=tuple(out_shape),
        in_specs=in_specs,
        out_specs=tuple(out_specs),
        scratch_shapes=scratch,
        compiler_params=pltpu.CompilerParams(collective_id=collective_id, has_side_effects=True),
        cost_estimate=pl.CostEstimate(flops=0, transcendentals=0, bytes_accessed=moved),
    )(*operands)
    gathered = [g.reshape((n_tok * g.shape[2],) + g.shape[3:]) for g in results[:n_in]]
    if n_grp:
        return gathered, results[n_in]
    return gathered

def layer_sum(summand, base_full):
    return lax.psum(summand.astype(jnp.bfloat16), "grp").astype(jnp.float32) + base_full


def normed_rows(stream, gain_vec):
    scaled = rms_scale(stream, gain_vec)
    return scaled.reshape(-1, scaled.shape[-1])


def shards(
    hidden,
    draft_qkv,
    self_cache,
    cross_cache,
    parents,
    counts,
    self_len,
    enc_len,
    buckets,
    bias_table,
    gain_cross,
    gain_ffn,
    gain_next,
    w_out_self,
    w_query_cross,
    w_out_cross,
    w_gate,
    w_up,
    w_down,
    w_qkv,
):
    requests, share_rows, model_width = hidden.shape
    draft_slots = draft_qkv.shape[2]
    head_width = draft_qkv.shape[3]
    self_context = draft_attention(
        draft_qkv, self_cache, parents, counts, self_len, buckets, bias_table
    )
    (w_out_self_t,) = fetch_group(lax.axis_size("tok"), 3, (w_out_self.T,), self_context)
    partial_value = jnp.einsum(
        "rk,ok->ro", self_context, w_out_self_t, preferred_element_type=jnp.float32
    )
    partial_value = partial_value.reshape(requests, draft_slots, model_width)
    own_rows = hidden.astype(jnp.float32)
    offset = lax.axis_index("grp") * share_rows
    placed = lax.dynamic_update_slice(
        jnp.zeros((requests, draft_slots, model_width), jnp.float32), own_rows, (0, offset, 0)
    )
    summand = partial_value + placed
    n_tok = lax.axis_size("tok")
    (w_query_full, w_out_cross_t, w_gate_full), summed = fetch_group(
        n_tok, 0, (w_query_cross, w_out_cross.T, w_gate), None, summand.astype(jnp.bfloat16)
    )
    stream_one = summed.astype(jnp.float32)
    normed_one = normed_rows(stream_one, gain_cross)
    cross_query = jnp.dot(normed_one, w_query_full, preferred_element_type=jnp.float32)
    cross_query = cross_query.astype(jnp.bfloat16).reshape(requests, draft_slots, head_width)
    cross_context = cross_attention_kernel(cross_query, cross_cache, enc_len)
    partial_value = jnp.einsum(
        "rk,ok->ro", cross_context, w_out_cross_t, preferred_element_type=jnp.float32
    )
    (w_up_full, w_down_t), summed = fetch_group(
        n_tok, 1, (w_up, w_down.T), None,
        partial_value.reshape(requests, draft_slots, model_width).astype(jnp.bfloat16),
    )
    stream_two = summed.astype(jnp.float32) + stream_one
    normed_two = normed_rows(stream_two, gain_ffn)
    gate_part = jnp.dot(normed_two, w_gate_full, preferred_element_type=jnp.float32)
    up_part = jnp.dot(normed_two, w_up_full, preferred_element_type=jnp.float32)
    gated = (jax.nn.gelu(gate_part, approximate=True) * up_part).astype(jnp.bfloat16)
    partial_value = jnp.einsum("rk,ok->ro", gated, w_down_t, preferred_element_type=jnp.float32)
    (w_qkv_full,), summed = fetch_group(
        n_tok, 2, (w_qkv.reshape(w_qkv.shape[0], -1),), None,
        partial_value.reshape(requests, draft_slots, model_width).astype(jnp.bfloat16),
    )
    stream_three = summed.astype(jnp.float32) + stream_two
    normed_three = normed_rows(stream_three, gain_next)
    projected = jnp.dot(
        normed_three,
        w_qkv_full.reshape(w_qkv_full.shape[0], -1),
        preferred_element_type=jnp.float32,
    )
    projected = projected.astype(jnp.bfloat16).reshape(requests, draft_slots, 3, head_width)
    next_qkv = jnp.transpose(projected, (2, 0, 1, 3))
    out_hidden = lax.dynamic_slice_in_dim(stream_three, offset, share_rows, 1).astype(jnp.bfloat16)
    return (out_hidden, next_qkv)


def solution(mesh):
    in_specs = (
        P("tok", "grp", None),
        P(None, "tok", None, "grp"),
        P("tok", None, None, "grp"),
        P("tok", None, None, "grp"),
        P("tok", None),
        P("tok"),
        P("tok"),
        P("tok"),
        P("tok", None, None),
        P(None, "grp"),
        P(),
        P(),
        P(),
        P("grp", "tok"),
        P("tok", "grp"),
        P("grp", "tok"),
        P("tok", "grp"),
        P("tok", "grp"),
        P("grp", "tok"),
        P("tok", None, "grp"),
    )
    out_specs = (P("tok", "grp", None), P(None, "tok", None, "grp"))
    return jax.shard_map(shards, mesh=mesh, in_specs=in_specs, out_specs=out_specs, check_vma=False)
```

```python
import functools

import jax
import jax.numpy as jnp
from jax import lax
from jax.experimental import pallas as pl
from jax.experimental.pallas import tpu as pltpu
from jax.sharding import PartitionSpec as P

DH = 64


def ancestor_table(parent_ids):
    count_slots = parent_ids.shape[0]
    slot_ids = jnp.arange(count_slots, dtype=jnp.int32)
    ancestors = jnp.eye(count_slots, dtype=jnp.float32) + (
        parent_ids[:, None] == slot_ids[None, :]
    ).astype(jnp.float32)
    for repeat in range(max(1, count_slots.bit_length())):
        ancestors = jnp.minimum(jnp.dot(ancestors, ancestors, precision=lax.Precision.HIGHEST), 1.0)
    return ancestors


def rms_scale(stream, gain_vec):
    mean_square = jnp.mean(stream * stream, axis=-1, keepdims=True)
    return (stream * lax.rsqrt(mean_square + 1e-06) * gain_vec).astype(jnp.bfloat16)


def draft_attention(projected, cached, parent_ids, draft_count, length, bucket_ids, bias_table):
    requests, draft_slots, head_width = (projected.shape[1], projected.shape[2], projected.shape[3])
    local_heads = bias_table.shape[1]
    head_size = head_width // local_heads
    queries = projected[0].reshape(requests, draft_slots, local_heads, head_size)
    draft_keys = projected[1].reshape(requests, draft_slots, local_heads, head_size)
    draft_values = projected[2].reshape(requests, draft_slots, local_heads, head_size)
    cache_keys = cached[:, 0].reshape(requests, -1, local_heads, head_size)
    cache_values = cached[:, 1].reshape(requests, -1, local_heads, head_size)
    cache_scores = jnp.einsum(
        "rihd,rphd->rhip", queries, cache_keys, preferred_element_type=jnp.float32
    )
    cache_scores = cache_scores + bias_table[-1][None, :, None, None]
    cache_live = jnp.arange(cache_keys.shape[1], dtype=jnp.int32)[None, :] < length[:, None]
    cache_scores = jnp.where(cache_live[:, None, None, :], cache_scores, -1e30)
    onehot = (bucket_ids[..., None] == jnp.arange(bias_table.shape[0], dtype=jnp.int32)).astype(
        jnp.float32
    )
    draft_bias = jnp.einsum("rijb,bh->rhij", onehot, bias_table, precision=lax.Precision.HIGHEST)
    draft_scores = (
        jnp.einsum("rihd,rjhd->rhij", queries, draft_keys, preferred_element_type=jnp.float32)
        + draft_bias
    )
    ancestors = jax.vmap(ancestor_table)(parent_ids)
    draft_live = (ancestors > 0.5) & (
        jnp.arange(draft_slots, dtype=jnp.int32)[None, None, :] < draft_count[:, None, None]
    )
    draft_scores = jnp.where(draft_live[:, None], draft_scores, -1e30)
    highest = jnp.maximum(cache_scores.max(-1, keepdims=True), draft_scores.max(-1, keepdims=True))
    exp_cache = jnp.exp(cache_scores - highest)
    exp_draft = jnp.exp(draft_scores - highest)
    denominator = exp_cache.sum(-1, keepdims=True) + exp_draft.sum(-1, keepdims=True)
    weights_cache = (exp_cache / denominator).astype(jnp.bfloat16)
    weights_draft = (exp_draft / denominator).astype(jnp.bfloat16)
    attended = jnp.einsum(
        "rhip,rphd->rihd", weights_cache, cache_values, preferred_element_type=jnp.float32
    )
    attended = attended + jnp.einsum(
        "rhij,rjhd->rihd", weights_draft, draft_values, preferred_element_type=jnp.float32
    )
    return attended.astype(jnp.bfloat16).reshape(requests * draft_slots, head_width)


def cross_attention(query_rows, cached, length):
    requests, draft_slots, head_width = query_rows.shape
    local_heads = head_width // DH
    queries = query_rows.reshape(requests, draft_slots, local_heads, DH)
    enc_keys = cached[:, 0].reshape(requests, -1, local_heads, DH)
    enc_values = cached[:, 1].reshape(requests, -1, local_heads, DH)
    scores = jnp.einsum("rihd,rphd->rhip", queries, enc_keys, preferred_element_type=jnp.float32)
    live = jnp.arange(enc_keys.shape[1], dtype=jnp.int32)[None, :] < length[:, None]
    scores = jnp.where(live[:, None, None, :], scores, -1e30)
    highest = scores.max(-1, keepdims=True)
    exp_scores = jnp.exp(scores - highest)
    weights = (exp_scores / exp_scores.sum(-1, keepdims=True)).astype(jnp.bfloat16)
    attended = jnp.einsum(
        "rhip,rphd->rihd", weights, enc_values, preferred_element_type=jnp.float32
    )
    return attended.astype(jnp.bfloat16).reshape(requests * draft_slots, head_width)


def cross_kernel(len_ref, q_ref, kv_ref, o_ref):
    length = len_ref[pl.program_id(0)]
    q = q_ref[0]
    keys = kv_ref[0, 0]
    values = kv_ref[0, 1]
    live = lax.broadcasted_iota(jnp.int32, (q.shape[0], keys.shape[0]), 1) < length
    head_of = lax.broadcasted_iota(jnp.int32, q.shape, 1) // DH
    result = jnp.zeros(q.shape, jnp.float32)
    for h in range(q.shape[1] // DH):
        own = head_of == h
        scores = lax.dot_general(
            jnp.where(own, q, jnp.zeros_like(q)), keys, (((1,), (1,)), ((), ())),
            preferred_element_type=jnp.float32,
        )
        scores = jnp.where(live, scores, -1e30)
        exp_scores = jnp.exp(scores - scores.max(-1, keepdims=True))
        total = exp_scores.sum(-1, keepdims=True)
        unscaled = jnp.dot(
            exp_scores.astype(jnp.bfloat16), values, preferred_element_type=jnp.float32
        )
        result = jnp.where(own, unscaled / total, result)
    o_ref[0] = result.astype(o_ref.dtype)

def cross_attention_kernel(query_rows, cached, length):
    requests, draft_slots, head_width = query_rows.shape
    positions = cached.shape[2]
    attended = pl.pallas_call(
        cross_kernel,
        out_shape=jax.ShapeDtypeStruct(query_rows.shape, jnp.bfloat16),
        grid_spec=pltpu.PrefetchScalarGridSpec(
            num_scalar_prefetch=1,
            grid=(requests,),
            in_specs=[
                pl.BlockSpec((1, draft_slots, head_width), lambda r, lens: (r, 0, 0)),
                pl.BlockSpec((1, 2, positions, head_width), lambda r, lens: (r, 0, 0, 0)),
            ],
            out_specs=pl.BlockSpec((1, draft_slots, head_width), lambda r, lens: (r, 0, 0)),
        ),
        cost_estimate=pl.CostEstimate(
            flops=4 * requests * draft_slots * positions * head_width,
            transcendentals=requests * draft_slots * positions * (head_width // DH),
            bytes_accessed=2 * cached.size + 4 * query_rows.size,
        ),
    )(length, query_rows, cached)
    return attended.reshape(requests * draft_slots, head_width)


def gather_kernel(n_chips, n_in, n_grp, *refs):
    srcs = refs[:n_in]
    if n_grp:
        summand = refs[n_in]
        outs = refs[n_in + 1:2 * n_in + 1]
        summed = refs[2 * n_in + 1]
        rest = refs[2 * n_in + 2:]
        send_sems, recv_sems, local_sems, fwd_send, fwd_recv, parts_in, rs_send, rs_recv, ag_send, ag_recv = rest
    else:
        outs = refs[n_in:2 * n_in]
        send_sems, recv_sems, local_sems, fwd_send, fwd_recv = refs[2 * n_in:]
    grp = lax.axis_index("grp")
    me = lax.axis_index("tok")
    chip = me // 2
    core = me % 2
    sibling = chip * 2 + (1 - core)
    mesh_id = pl.DeviceIdType.MESH

    barrier = pltpu.get_barrier_semaphore()
    for k in range(1, n_chips):
        peer = lax.rem(chip + k, n_chips) * 2 + core
        pl.semaphore_signal(barrier, inc=1, device_id=(grp, peer), device_id_type=mesh_id)
    pl.semaphore_signal(barrier, inc=1, device_id=(grp, sibling), device_id_type=mesh_id)
    for j in range(1, max(n_grp, 1)):
        pl.semaphore_signal(
            barrier, inc=1, device_id=(lax.rem(grp + j, n_grp), me), device_id_type=mesh_id
        )
    pl.semaphore_wait(barrier, n_chips + max(n_grp - 1, 0))

    locals_ = [
        pltpu.make_async_copy(srcs[i], outs[i].at[chip, core], local_sems.at[i]) for i in range(n_in)
    ]
    for copy in locals_:
        copy.start()

    def remote(i, k):
        other = lax.rem(chip + k, n_chips)
        return pltpu.make_async_remote_copy(
            src_ref=srcs[i],
            dst_ref=outs[i].at[chip, core],
            send_sem=send_sems.at[i, k],
            recv_sem=recv_sems.at[i, chip],
            device_id=(grp, other * 2 + core),
            device_id_type=mesh_id,
        )

    def send(k, carry):
        for i in range(n_in):
            remote(i, k).start()
        return carry

    lax.fori_loop(1, n_chips, send, 0)

    if n_grp:
        quarter = summand.shape[1] // n_grp

        def scatter(j):
            target = lax.rem(grp + j, n_grp)
            return pltpu.make_async_remote_copy(
                src_ref=summand.at[:, pl.ds(target * quarter, quarter)],
                dst_ref=parts_in.at[grp],
                send_sem=rs_send.at[j],
                recv_sem=rs_recv.at[grp],
                device_id=(target, me),
                device_id_type=mesh_id,
            )

        for j in range(1, n_grp):
            scatter(j).start()
        for j in range(1, n_grp):
            scatter(j).wait_send()
            source = lax.rem(grp + j, n_grp)
            pltpu.make_async_copy(parts_in.at[source], parts_in.at[source], rs_recv.at[source]).wait()
        mine = pl.ds(grp * quarter, quarter)
        total = summand[:, mine, :].astype(jnp.float32)
        for j in range(1, n_grp):
            total = total + parts_in[lax.rem(grp + j, n_grp)].astype(jnp.float32)
        summed[:, mine, :] = total.astype(summed.dtype)

        def spread(j):
            target = lax.rem(grp + j, n_grp)
            return pltpu.make_async_remote_copy(
                src_ref=summed.at[:, mine],
                dst_ref=summed.at[:, mine],
                send_sem=ag_send.at[j],
                recv_sem=ag_recv.at[grp],
                device_id=(target, me),
                device_id_type=mesh_id,
            )

        for j in range(1, n_grp):
            spread(j).start()

    def forward(i, c):
        return pltpu.make_async_remote_copy(
            src_ref=outs[i].at[c, core],
            dst_ref=outs[i].at[c, core],
            send_sem=fwd_send.at[i, c],
            recv_sem=fwd_recv.at[i, c],
            device_id=(grp, sibling),
            device_id_type=mesh_id,
        )

    for i in range(n_in):
        locals_[i].wait()
        forward(i, chip).start()

    def arrive(k, carry):
        other = lax.rem(chip + k, n_chips)
        for i in range(n_in):
            pltpu.make_async_copy(
                srcs[i], outs[i].at[other, core], recv_sems.at[i, other]
            ).wait()
            forward(i, other).start()
        for i in range(n_in):
            remote(i, k).wait_send()
        return carry

    lax.fori_loop(1, n_chips, arrive, 0)

    def land(c, carry):
        for i in range(n_in):
            forward(i, c).wait_send()
            pltpu.make_async_copy(
                outs[i].at[c, core], outs[i].at[c, 1 - core], fwd_recv.at[i, c]
            ).wait()
        return carry

    lax.fori_loop(0, n_chips, land, 0)

    if n_grp:
        for j in range(1, n_grp):
            spread(j).wait_send()
            source = lax.rem(grp + j, n_grp)
            rows = pl.ds(source * quarter, quarter)
            pltpu.make_async_copy(summed.at[:, rows], summed.at[:, rows], ag_recv.at[source]).wait()


def fetch_group(n_tok, collective_id, parts, after, summand=None):
    if summand is None:
        parts = list(lax.optimization_barrier((tuple(parts), after))[0])
    n_chips = n_tok // 2
    n_in = len(parts)
    n_grp = 0 if summand is None else lax.axis_size("grp")
    moved = 2 * n_tok * sum(p.size for p in parts) * parts[0].dtype.itemsize
    out_shape = [jax.ShapeDtypeStruct((n_chips, 2) + p.shape, p.dtype) for p in parts]
    out_specs = [pl.BlockSpec(memory_space=pl.ANY) for _ in parts]
    in_specs = [pl.BlockSpec(memory_space=pl.ANY)] * n_in
    operands = list(parts)
    scratch = [
        pltpu.SemaphoreType.DMA((n_in, n_chips)),
        pltpu.SemaphoreType.DMA((n_in, n_chips)),
        pltpu.SemaphoreType.DMA((n_in,)),
        pltpu.SemaphoreType.DMA((n_in, n_chips)),
        pltpu.SemaphoreType.DMA((n_in, n_chips)),
    ]
    if n_grp:
        requests, slots, width = summand.shape
        operands.append(summand)
        in_specs.append(pl.BlockSpec(memory_space=pltpu.VMEM))
        out_shape.append(jax.ShapeDtypeStruct(summand.shape, summand.dtype))
        out_specs.append(pl.BlockSpec(memory_space=pltpu.VMEM))
        scratch += [
            pltpu.VMEM((n_grp, requests, slots // n_grp, width), summand.dtype),
            pltpu.SemaphoreType.DMA((n_grp,)),
            pltpu.SemaphoreType.DMA((n_grp,)),
            pltpu.SemaphoreType.DMA((n_grp,)),
            pltpu.SemaphoreType.DMA((n_grp,)),
        ]
    results = pl.pallas_call(
        functools.partial(gather_kernel, n_chips, n_in, n_grp),
        out_shape=tuple(out_shape),
        in_specs=in_specs,
        out_specs=tuple(out_specs),
        scratch_shapes=scratch,
        compiler_params=pltpu.CompilerParams(collective_id=collective_id, has_side_effects=True),
        cost_estimate=pl.CostEstimate(flops=0, transcendentals=0, bytes_accessed=moved),
    )(*operands)
    gathered = [g.reshape((n_tok * g.shape[2],) + g.shape[3:]) for g in results[:n_in]]
    if n_grp:
        return gathered, results[n_in]
    return gathered

def layer_sum(summand, base_full):
    return lax.psum(summand.astype(jnp.bfloat16), "grp").astype(jnp.float32) + base_full


def normed_rows(stream, gain_vec):
    scaled = rms_scale(stream, gain_vec)
    return scaled.reshape(-1, scaled.shape[-1])


def shards(
    hidden,
    draft_qkv,
    self_cache,
    cross_cache,
    parents,
    counts,
    self_len,
    enc_len,
    buckets,
    bias_table,
    gain_cross,
    gain_ffn,
    gain_next,
    w_out_self,
    w_query_cross,
    w_out_cross,
    w_gate,
    w_up,
    w_down,
    w_qkv,
):
    requests, share_rows, model_width = hidden.shape
    draft_slots = draft_qkv.shape[2]
    head_width = draft_qkv.shape[3]
    self_context = draft_attention(
        draft_qkv, self_cache, parents, counts, self_len, buckets, bias_table
    )
    (w_out_self_t,) = fetch_group(lax.axis_size("tok"), 3, (w_out_self.T,), self_context)
    partial_value = jnp.einsum(
        "rk,ok->ro", self_context, w_out_self_t, preferred_element_type=jnp.float32
    )
    partial_value = partial_value.reshape(requests, draft_slots, model_width)
    own_rows = hidden.astype(jnp.float32)
    offset = lax.axis_index("grp") * share_rows
    placed = lax.dynamic_update_slice(
        jnp.zeros((requests, draft_slots, model_width), jnp.float32), own_rows, (0, offset, 0)
    )
    summand = partial_value + placed
    n_tok = lax.axis_size("tok")
    (w_query_full, w_out_cross_t, w_gate_full), summed = fetch_group(
        n_tok, 0, (w_query_cross, w_out_cross.T, w_gate), None, summand.astype(jnp.bfloat16)
    )
    stream_one = summed.astype(jnp.float32)
    normed_one = normed_rows(stream_one, gain_cross)
    cross_query = jnp.dot(normed_one, w_query_full, preferred_element_type=jnp.float32)
    cross_query = cross_query.astype(jnp.bfloat16).reshape(requests, draft_slots, head_width)
    cross_context = cross_attention_kernel(cross_query, cross_cache, enc_len)
    partial_value = jnp.einsum(
        "rk,ok->ro", cross_context, w_out_cross_t, preferred_element_type=jnp.float32
    )
    (w_up_full, w_down_t), summed = fetch_group(
        n_tok, 1, (w_up, w_down.T), None,
        partial_value.reshape(requests, draft_slots, model_width).astype(jnp.bfloat16),
    )
    stream_two = summed.astype(jnp.float32) + stream_one
    normed_two = normed_rows(stream_two, gain_ffn)
    gate_part = jnp.dot(normed_two, w_gate_full, preferred_element_type=jnp.float32)
    up_part = jnp.dot(normed_two, w_up_full, preferred_element_type=jnp.float32)
    gated = (jax.nn.gelu(gate_part, approximate=True) * up_part).astype(jnp.bfloat16)
    partial_value = jnp.einsum("rk,ok->ro", gated, w_down_t, preferred_element_type=jnp.float32)
    (w_qkv_full,), summed = fetch_group(
        n_tok, 2, (w_qkv.reshape(w_qkv.shape[0], -1),), None,
        partial_value.reshape(requests, draft_slots, model_width).astype(jnp.bfloat16),
    )
    stream_three = summed.astype(jnp.float32) + stream_two
    normed_three = normed_rows(stream_three, gain_next)
    projected = jnp.dot(
        normed_three,
        w_qkv_full.reshape(w_qkv_full.shape[0], -1),
        preferred_element_type=jnp.float32,
    )
    projected = projected.astype(jnp.bfloat16).reshape(requests, draft_slots, 3, head_width)
    next_qkv = jnp.transpose(projected, (2, 0, 1, 3))
    out_hidden = lax.dynamic_slice_in_dim(stream_three, offset, share_rows, 1).astype(jnp.bfloat16)
    return (out_hidden, next_qkv)


def solution(mesh):
    in_specs = (
        P("tok", "grp", None),
        P(None, "tok", None, "grp"),
        P("tok", None, None, "grp"),
        P("tok", None, None, "grp"),
        P("tok", None),
        P("tok"),
        P("tok"),
        P("tok"),
        P("tok", None, None),
        P(None, "grp"),
        P(),
        P(),
        P(),
        P("grp", "tok"),
        P("tok", "grp"),
        P("grp", "tok"),
        P("tok", "grp"),
        P("tok", "grp"),
        P("grp", "tok"),
        P("tok", None, "grp"),
    )
    out_specs = (P("tok", "grp", None), P(None, "tok", None, "grp"))
    return jax.shard_map(shards, mesh=mesh, in_specs=in_specs, out_specs=out_specs, check_vma=False)
```

```python
import functools

import jax
import jax.numpy as jnp
from jax import lax
from jax.experimental import pallas as pl
from jax.experimental.pallas import tpu as pltpu
from jax.sharding import PartitionSpec as P

DH = 64


def ancestor_table(parent_ids):
    count_slots = parent_ids.shape[0]
    slot_ids = jnp.arange(count_slots, dtype=jnp.int32)
    ancestors = jnp.eye(count_slots, dtype=jnp.float32) + (
        parent_ids[:, None] == slot_ids[None, :]
    ).astype(jnp.float32)
    for repeat in range(max(1, count_slots.bit_length())):
        ancestors = jnp.minimum(jnp.dot(ancestors, ancestors, precision=lax.Precision.HIGHEST), 1.0)
    return ancestors


def rms_scale(stream, gain_vec):
    mean_square = jnp.mean(stream * stream, axis=-1, keepdims=True)
    return (stream * lax.rsqrt(mean_square + 1e-06) * gain_vec).astype(jnp.bfloat16)


def draft_attention(projected, cached, parent_ids, draft_count, length, bucket_ids, bias_table):
    requests, draft_slots, head_width = (projected.shape[1], projected.shape[2], projected.shape[3])
    local_heads = bias_table.shape[1]
    head_size = head_width // local_heads
    queries = projected[0].reshape(requests, draft_slots, local_heads, head_size)
    draft_keys = projected[1].reshape(requests, draft_slots, local_heads, head_size)
    draft_values = projected[2].reshape(requests, draft_slots, local_heads, head_size)
    cache_keys = cached[:, 0].reshape(requests, -1, local_heads, head_size)
    cache_values = cached[:, 1].reshape(requests, -1, local_heads, head_size)
    cache_scores = jnp.einsum(
        "rihd,rphd->rhip", queries, cache_keys, preferred_element_type=jnp.float32
    )
    cache_scores = cache_scores + bias_table[-1][None, :, None, None]
    cache_live = jnp.arange(cache_keys.shape[1], dtype=jnp.int32)[None, :] < length[:, None]
    cache_scores = jnp.where(cache_live[:, None, None, :], cache_scores, -1e30)
    onehot = (bucket_ids[..., None] == jnp.arange(bias_table.shape[0], dtype=jnp.int32)).astype(
        jnp.float32
    )
    draft_bias = jnp.einsum("rijb,bh->rhij", onehot, bias_table, precision=lax.Precision.HIGHEST)
    draft_scores = (
        jnp.einsum("rihd,rjhd->rhij", queries, draft_keys, preferred_element_type=jnp.float32)
        + draft_bias
    )
    ancestors = jax.vmap(ancestor_table)(parent_ids)
    draft_live = (ancestors > 0.5) & (
        jnp.arange(draft_slots, dtype=jnp.int32)[None, None, :] < draft_count[:, None, None]
    )
    draft_scores = jnp.where(draft_live[:, None], draft_scores, -1e30)
    highest = jnp.maximum(cache_scores.max(-1, keepdims=True), draft_scores.max(-1, keepdims=True))
    exp_cache = jnp.exp(cache_scores - highest)
    exp_draft = jnp.exp(draft_scores - highest)
    denominator = exp_cache.sum(-1, keepdims=True) + exp_draft.sum(-1, keepdims=True)
    weights_cache = (exp_cache / denominator).astype(jnp.bfloat16)
    weights_draft = (exp_draft / denominator).astype(jnp.bfloat16)
    attended = jnp.einsum(
        "rhip,rphd->rihd", weights_cache, cache_values, preferred_element_type=jnp.float32
    )
    attended = attended + jnp.einsum(
        "rhij,rjhd->rihd", weights_draft, draft_values, preferred_element_type=jnp.float32
    )
    return attended.astype(jnp.bfloat16).reshape(requests * draft_slots, head_width)


def cross_attention(query_rows, cached, length):
    requests, draft_slots, head_width = query_rows.shape
    local_heads = head_width // DH
    queries = query_rows.reshape(requests, draft_slots, local_heads, DH)
    enc_keys = cached[:, 0].reshape(requests, -1, local_heads, DH)
    enc_values = cached[:, 1].reshape(requests, -1, local_heads, DH)
    scores = jnp.einsum("rihd,rphd->rhip", queries, enc_keys, preferred_element_type=jnp.float32)
    live = jnp.arange(enc_keys.shape[1], dtype=jnp.int32)[None, :] < length[:, None]
    scores = jnp.where(live[:, None, None, :], scores, -1e30)
    highest = scores.max(-1, keepdims=True)
    exp_scores = jnp.exp(scores - highest)
    weights = (exp_scores / exp_scores.sum(-1, keepdims=True)).astype(jnp.bfloat16)
    attended = jnp.einsum(
        "rhip,rphd->rihd", weights, enc_values, preferred_element_type=jnp.float32
    )
    return attended.astype(jnp.bfloat16).reshape(requests * draft_slots, head_width)


def gather_kernel(n_chips, n_in, n_grp, *refs):
    srcs = refs[:n_in]
    if n_grp:
        summand = refs[n_in]
        outs = refs[n_in + 1:2 * n_in + 1]
        summed = refs[2 * n_in + 1]
        rest = refs[2 * n_in + 2:]
        send_sems, recv_sems, local_sems, fwd_send, fwd_recv, parts_in, rs_send, rs_recv, ag_send, ag_recv = rest
    else:
        outs = refs[n_in:2 * n_in]
        send_sems, recv_sems, local_sems, fwd_send, fwd_recv = refs[2 * n_in:]
    grp = lax.axis_index("grp")
    me = lax.axis_index("tok")
    chip = me // 2
    core = me % 2
    sibling = chip * 2 + (1 - core)
    mesh_id = pl.DeviceIdType.MESH

    barrier = pltpu.get_barrier_semaphore()
    for k in range(1, n_chips):
        peer = lax.rem(chip + k, n_chips) * 2 + core
        pl.semaphore_signal(barrier, inc=1, device_id=(grp, peer), device_id_type=mesh_id)
    pl.semaphore_signal(barrier, inc=1, device_id=(grp, sibling), device_id_type=mesh_id)
    for j in range(1, max(n_grp, 1)):
        pl.semaphore_signal(
            barrier, inc=1, device_id=(lax.rem(grp + j, n_grp), me), device_id_type=mesh_id
        )
    pl.semaphore_wait(barrier, n_chips + max(n_grp - 1, 0))

    locals_ = [
        pltpu.make_async_copy(srcs[i], outs[i].at[chip, core], local_sems.at[i]) for i in range(n_in)
    ]
    for copy in locals_:
        copy.start()

    def remote(i, k):
        other = lax.rem(chip + k, n_chips)
        return pltpu.make_async_remote_copy(
            src_ref=srcs[i],
            dst_ref=outs[i].at[chip, core],
            send_sem=send_sems.at[i, k],
            recv_sem=recv_sems.at[i, chip],
            device_id=(grp, other * 2 + core),
            device_id_type=mesh_id,
        )

    if n_grp:
        quarter = summand.shape[1] // n_grp

        def scatter(j):
            target = lax.rem(grp + j, n_grp)
            return pltpu.make_async_remote_copy(
                src_ref=summand.at[:, pl.ds(target * quarter, quarter)],
                dst_ref=parts_in.at[grp],
                send_sem=rs_send.at[j],
                recv_sem=rs_recv.at[grp],
                device_id=(target, me),
                device_id_type=mesh_id,
            )

        for j in range(1, n_grp):
            scatter(j).start()
    def send(k, carry):
        for i in range(n_in):
            remote(i, k).start()
        return carry

    lax.fori_loop(1, n_chips, send, 0)

    if n_grp:
        for j in range(1, n_grp):
            scatter(j).wait_send()
            source = lax.rem(grp + j, n_grp)
            pltpu.make_async_copy(parts_in.at[source], parts_in.at[source], rs_recv.at[source]).wait()
        mine = pl.ds(grp * quarter, quarter)
        total = summand[:, mine, :].astype(jnp.float32)
        for j in range(1, n_grp):
            total = total + parts_in[lax.rem(grp + j, n_grp)].astype(jnp.float32)
        summed[:, mine, :] = total.astype(summed.dtype)

        def spread(j):
            target = lax.rem(grp + j, n_grp)
            return pltpu.make_async_remote_copy(
                src_ref=summed.at[:, mine],
                dst_ref=summed.at[:, mine],
                send_sem=ag_send.at[j],
                recv_sem=ag_recv.at[grp],
                device_id=(target, me),
                device_id_type=mesh_id,
            )

        for j in range(1, n_grp):
            spread(j).start()

    def forward(i, c):
        return pltpu.make_async_remote_copy(
            src_ref=outs[i].at[c, core],
            dst_ref=outs[i].at[c, core],
            send_sem=fwd_send.at[i, c],
            recv_sem=fwd_recv.at[i, c],
            device_id=(grp, sibling),
            device_id_type=mesh_id,
        )

    for i in range(n_in):
        locals_[i].wait()
        forward(i, chip).start()

    def arrive(k, carry):
        other = lax.rem(chip + k, n_chips)
        for i in range(n_in):
            pltpu.make_async_copy(
                srcs[i], outs[i].at[other, core], recv_sems.at[i, other]
            ).wait()
            forward(i, other).start()
        for i in range(n_in):
            remote(i, k).wait_send()
        return carry

    lax.fori_loop(1, n_chips, arrive, 0)

    def land(c, carry):
        for i in range(n_in):
            forward(i, c).wait_send()
            pltpu.make_async_copy(
                outs[i].at[c, core], outs[i].at[c, 1 - core], fwd_recv.at[i, c]
            ).wait()
        return carry

    lax.fori_loop(0, n_chips, land, 0)

    if n_grp:
        for j in range(1, n_grp):
            spread(j).wait_send()
            source = lax.rem(grp + j, n_grp)
            rows = pl.ds(source * quarter, quarter)
            pltpu.make_async_copy(summed.at[:, rows], summed.at[:, rows], ag_recv.at[source]).wait()


def fetch_group(n_tok, collective_id, parts, after, summand=None):
    if summand is None:
        parts = list(lax.optimization_barrier((tuple(parts), after))[0])
    n_chips = n_tok // 2
    n_in = len(parts)
    n_grp = 0 if summand is None else lax.axis_size("grp")
    moved = 2 * n_tok * sum(p.size for p in parts) * parts[0].dtype.itemsize
    out_shape = [jax.ShapeDtypeStruct((n_chips, 2) + p.shape, p.dtype) for p in parts]
    out_specs = [pl.BlockSpec(memory_space=pl.ANY) for _ in parts]
    in_specs = [pl.BlockSpec(memory_space=pl.ANY)] * n_in
    operands = list(parts)
    scratch = [
        pltpu.SemaphoreType.DMA((n_in, n_chips)),
        pltpu.SemaphoreType.DMA((n_in, n_chips)),
        pltpu.SemaphoreType.DMA((n_in,)),
        pltpu.SemaphoreType.DMA((n_in, n_chips)),
        pltpu.SemaphoreType.DMA((n_in, n_chips)),
    ]
    if n_grp:
        requests, slots, width = summand.shape
        operands.append(summand)
        in_specs.append(pl.BlockSpec(memory_space=pltpu.VMEM))
        out_shape.append(jax.ShapeDtypeStruct(summand.shape, summand.dtype))
        out_specs.append(pl.BlockSpec(memory_space=pltpu.VMEM))
        scratch += [
            pltpu.VMEM((n_grp, requests, slots // n_grp, width), summand.dtype),
            pltpu.SemaphoreType.DMA((n_grp,)),
            pltpu.SemaphoreType.DMA((n_grp,)),
            pltpu.SemaphoreType.DMA((n_grp,)),
            pltpu.SemaphoreType.DMA((n_grp,)),
        ]
    results = pl.pallas_call(
        functools.partial(gather_kernel, n_chips, n_in, n_grp),
        out_shape=tuple(out_shape),
        in_specs=in_specs,
        out_specs=tuple(out_specs),
        scratch_shapes=scratch,
        compiler_params=pltpu.CompilerParams(collective_id=collective_id, has_side_effects=True),
        cost_estimate=pl.CostEstimate(flops=0, transcendentals=0, bytes_accessed=moved),
    )(*operands)
    gathered = [g.reshape((n_tok * g.shape[2],) + g.shape[3:]) for g in results[:n_in]]
    if n_grp:
        return gathered, results[n_in]
    return gathered

def layer_sum(summand, base_full):
    return lax.psum(summand.astype(jnp.bfloat16), "grp").astype(jnp.float32) + base_full


def normed_rows(stream, gain_vec):
    scaled = rms_scale(stream, gain_vec)
    return scaled.reshape(-1, scaled.shape[-1])


def shards(
    hidden,
    draft_qkv,
    self_cache,
    cross_cache,
    parents,
    counts,
    self_len,
    enc_len,
    buckets,
    bias_table,
    gain_cross,
    gain_ffn,
    gain_next,
    w_out_self,
    w_query_cross,
    w_out_cross,
    w_gate,
    w_up,
    w_down,
    w_qkv,
):
    requests, share_rows, model_width = hidden.shape
    draft_slots = draft_qkv.shape[2]
    head_width = draft_qkv.shape[3]
    self_context = draft_attention(
        draft_qkv, self_cache, parents, counts, self_len, buckets, bias_table
    )
    (w_out_self_t,) = fetch_group(lax.axis_size("tok"), 3, (w_out_self.T,), self_context)
    partial_value = jnp.einsum(
        "rk,ok->ro", self_context, w_out_self_t, preferred_element_type=jnp.float32
    )
    partial_value = partial_value.reshape(requests, draft_slots, model_width)
    own_rows = hidden.astype(jnp.float32)
    offset = lax.axis_index("grp") * share_rows
    placed = lax.dynamic_update_slice(
        jnp.zeros((requests, draft_slots, model_width), jnp.float32), own_rows, (0, offset, 0)
    )
    summand = partial_value + placed
    n_tok = lax.axis_size("tok")
    (w_query_full, w_out_cross_t, w_gate_full), summed = fetch_group(
        n_tok, 0, (w_query_cross, w_out_cross.T, w_gate), None, summand.astype(jnp.bfloat16)
    )
    stream_one = summed.astype(jnp.float32)
    normed_one = normed_rows(stream_one, gain_cross)
    cross_query = jnp.dot(normed_one, w_query_full, preferred_element_type=jnp.float32)
    cross_query = cross_query.astype(jnp.bfloat16).reshape(requests, draft_slots, head_width)
    cross_context = cross_attention(cross_query, cross_cache, enc_len)
    partial_value = jnp.einsum(
        "rk,ok->ro", cross_context, w_out_cross_t, preferred_element_type=jnp.float32
    )
    (w_up_full, w_down_t), summed = fetch_group(
        n_tok, 1, (w_up, w_down.T), None,
        partial_value.reshape(requests, draft_slots, model_width).astype(jnp.bfloat16),
    )
    stream_two = summed.astype(jnp.float32) + stream_one
    normed_two = normed_rows(stream_two, gain_ffn)
    gate_part = jnp.dot(normed_two, w_gate_full, preferred_element_type=jnp.float32)
    up_part = jnp.dot(normed_two, w_up_full, preferred_element_type=jnp.float32)
    gated = (jax.nn.gelu(gate_part, approximate=True) * up_part).astype(jnp.bfloat16)
    partial_value = jnp.einsum("rk,ok->ro", gated, w_down_t, preferred_element_type=jnp.float32)
    (w_qkv_full,), summed = fetch_group(
        n_tok, 2, (w_qkv.reshape(w_qkv.shape[0], -1),), None,
        partial_value.reshape(requests, draft_slots, model_width).astype(jnp.bfloat16),
    )
    stream_three = summed.astype(jnp.float32) + stream_two
    normed_three = normed_rows(stream_three, gain_next)
    projected = jnp.dot(
        normed_three,
        w_qkv_full.reshape(w_qkv_full.shape[0], -1),
        preferred_element_type=jnp.float32,
    )
    projected = projected.astype(jnp.bfloat16).reshape(requests, draft_slots, 3, head_width)
    next_qkv = jnp.transpose(projected, (2, 0, 1, 3))
    out_hidden = lax.dynamic_slice_in_dim(stream_three, offset, share_rows, 1).astype(jnp.bfloat16)
    return (out_hidden, next_qkv)


def solution(mesh):
    in_specs = (
        P("tok", "grp", None),
        P(None, "tok", None, "grp"),
        P("tok", None, None, "grp"),
        P("tok", None, None, "grp"),
        P("tok", None),
        P("tok"),
        P("tok"),
        P("tok"),
        P("tok", None, None),
        P(None, "grp"),
        P(),
        P(),
        P(),
        P("grp", "tok"),
        P("tok", "grp"),
        P("grp", "tok"),
        P("tok", "grp"),
        P("tok", "grp"),
        P("grp", "tok"),
        P("tok", None, "grp"),
    )
    out_specs = (P("tok", "grp", None), P(None, "tok", None, "grp"))
    return jax.shard_map(shards, mesh=mesh, in_specs=in_specs, out_specs=out_specs, check_vma=False)
```
